32 devices in a mesh: dir: 4 (over x, core), chan: 8 (over z, y).
Axes of the slice: x: 2, y: 2, z: 4, core: 2. Of those that a mesh axis runs over, the one named last changes fastest.
Arguments:
- visibilities: float32 [8, 256, 2, 256], P('chan'), may hold values from -4 to 4, as said below
- station_uv: float32 [2, 256], replicated, may hold values from -50 to 50
- source_lm: float32 [2, 64, 32], P(None, 'dir'), may hold values from -0.1 to 0.1
- source_flux: float32 [64, 32], P('dir'), may hold values from 0.01 to 0.1
- band_offset: float32 [8], P('chan'), may hold values from -1 to 1, as said below
- gains_init: float32 [2, 64, 8, 256], P(None, 'dir', 'chan'), may hold values from -1 to 2
- duals_init: float32 [2, 64, 8, 256], P(None, 'dir', 'chan'), may hold values from -3 to 3
- poly_init: float32 [2, 64, 1024], P(None, 'dir'), may hold values from -3 to 3
- penalty: float32 [64], P('dir'), may hold values from 1 to 8
- harmonics: float32 [64, 225], replicated, may hold values from -0.75 to 0.75
- threshold: float32 [1], replicated, may hold values from 0.1 to 0.4
Outputs:
- gains_new: float32 [2, 64, 8, 256], P(None, 'dir', 'chan')
- duals_new: float32 [2, 64, 8, 256], P(None, 'dir', 'chan')
- consensus: float32 [2, 64, 1024], P(None, 'dir')
The draws below stay inside these ranges and needn't reach their ends.
Inputs may be any that keep to these rules, and one draw needn't show every extreme that they name: visibilities[c, p, 0, q] = visibilities[c, q, 0, p] and visibilities[c, p, 1, q] = -visibilities[c, q, 1, p]. `band_offset`: strictly increasing.
All inputs are finite; a program needn't handle non-finite values.
Results may differ from the reference program's by a relative error of at most 0.0003.
Values sent between devices are 32-bit elements; how exact they have to be, the bound alone decides.
A program may use at most 64 MiB of HBM per device.

```python
import math
import jax
import jax.numpy as jnp
from jax import lax

S = 256
NSRC = 32
MODES = 225
NTERM = 4
SWEEPS = 2
K = 64
NCH = 8


def draw_band_offset(key, part):
    position = jnp.arange(NCH).astype(jnp.float32)
    jitter = jax.random.uniform(key, (NCH,), jnp.float32, -0.4, 0.4)
    return -1.0 + (2.0 * position + 1.0 + jitter) / NCH


def draw_gains_init(key, part):
    first_key, second_key = jax.random.split(key)
    dims = (K, NCH, S)
    real_part = 1.0 + 0.25 * jax.random.truncated_normal(first_key, -4.0, 4.0, dims, jnp.float32)
    imag_part = 0.25 * jax.random.truncated_normal(second_key, -4.0, 4.0, dims, jnp.float32)
    return jnp.stack([real_part, imag_part])


def draw_visibilities(key, part):
    first_key, second_key = jax.random.split(key)
    dims = (NCH, S, S)
    sym_draw = jax.random.truncated_normal(first_key, -4.0, 4.0, dims, jnp.float32)
    anti_draw = jax.random.truncated_normal(second_key, -4.0, 4.0, dims, jnp.float32)
    real_part = 0.5 * (sym_draw + jnp.swapaxes(sym_draw, 1, 2))
    imag_part = 0.5 * (anti_draw - jnp.swapaxes(anti_draw, 1, 2))
    return jnp.stack([real_part, imag_part], axis=2)


def level_of(key, extent, shards, smallest, largest):
    level, own = 1.0, jax.random.fold_in(key, 6)
    for dim, parts in shards:
        steps = jnp.exp(jax.random.uniform(jax.random.fold_in(own, dim), (parts,), jnp.float32, smallest / len(shards), largest / len(shards)))
        level = level * jnp.repeat(steps, extent[dim] // parts).reshape([-1 if axis == dim else 1 for axis in range(len(extent))])
    return level


def bell_draw(own_key, shape, deviation, reach, cuts=(), kind=jnp.bfloat16):
    drawn = deviation * jax.random.normal(own_key, shape, jnp.float32)
    if cuts:
        drawn = drawn * level_of(own_key, shape, cuts, -0.22, 0.18)
    return jnp.clip(drawn, -reach, reach).astype(kind)


def setup_inputs(seed: int = 0) -> dict:
    seeds = jax.random.split(jax.random.key(seed), 12)
    visibilities = draw_visibilities(jax.random.fold_in(seeds[11], 71), 0)
    station_uv = jnp.clip(jax.random.uniform(seeds[1], (2, S), jnp.float32, -50.0, 50.0), -50.0, 50.0)
    source_lm = jnp.clip(jax.random.uniform(seeds[2], (2, K, NSRC), jnp.float32, -0.1, 0.1) * level_of(seeds[2], (2, K, NSRC), ((1, 4),), -0.4, 0.0), -0.1, 0.1)
    source_flux = jnp.clip(jnp.exp(math.log(0.1) - 2.3025851 * jax.random.uniform(seeds[3], (K, NSRC), jnp.float32) ** level_of(seeds[3], (K, NSRC), ((0, 4),), -0.2, 0.2)), 0.01, 0.1)
    band_offset = draw_band_offset(jax.random.fold_in(seeds[11], 71), 0)
    gains_init = draw_gains_init(jax.random.fold_in(seeds[11], 71), 0)
    duals_init = bell_draw(seeds[6], (2, K, NCH, S), 0.5, 3.0, ((1, 4), (2, 8)), jnp.float32)
    poly_init = bell_draw(seeds[7], (2, K, S * NTERM), 0.5, 3.0, ((1, 4),), jnp.float32)
    penalty = jnp.clip(jnp.exp(math.log(8.0) - 2.0794415 * jax.random.uniform(seeds[8], (K,), jnp.float32) ** level_of(seeds[8], (K,), ((0, 4),), -0.2, 0.2)), 1.0, 8.0)
    harmonics = bell_draw(seeds[9], (K, MODES), K ** -0.5, 0.75, (), jnp.float32)
    threshold = jnp.clip(jax.random.uniform(seeds[10], (1,), jnp.float32, 0.1, 0.4), 0.1, 0.4)
    return dict(visibilities=visibilities, station_uv=station_uv, source_lm=source_lm, source_flux=source_flux, band_offset=band_offset, gains_init=gains_init, duals_init=duals_init, poly_init=poly_init, penalty=penalty, harmonics=harmonics, threshold=threshold)


highest_degree = lax.Precision.HIGHEST

def legendre(offset):
    return jnp.stack([jnp.ones_like(offset), offset, 0.5 * (3.0 * offset * offset - 1.0), 0.5 * (5.0 * offset * offset * offset - 3.0 * offset)], axis=0)

def gram_inverse(offsets):
    values = legendre(offsets)
    gram = jnp.dot(values, values.T, precision=highest_degree)
    factor = jnp.linalg.cholesky(gram)
    return jax.scipy.linalg.cho_solve((factor, True), jnp.eye(4, dtype=gram.dtype))

def phases(station_uv, source_lm, band_value):
    turns = 2.0 * math.pi * (1.0 + 0.25 * band_value)
    phase_arg = turns * (station_uv[0][:, None, None] * source_lm[0][None] + station_uv[1][:, None, None] * source_lm[1][None])
    return (jnp.cos(phase_arg), jnp.sin(phase_arg))

def refine(res_re, res_im, fringe_real, fringe_imaginary, flux_grp, start_re, start_im, goal_re, goal_im, weight):
    stations, groups, sources = fringe_real.shape
    weighted_real = fringe_real * flux_grp[None]
    weighted_imaginary = fringe_imaginary * flux_grp[None]
    coherency_real = jnp.einsum('ivd,gvd->vig', weighted_real, fringe_real, precision=highest_degree) + jnp.einsum('ivd,gvd->vig', weighted_imaginary, fringe_imaginary, precision=highest_degree)
    coherency_imaginary = jnp.einsum('ivd,gvd->vig', weighted_imaginary, fringe_real, precision=highest_degree) - jnp.einsum('ivd,gvd->vig', weighted_real, fringe_imaginary, precision=highest_degree)
    power_map = coherency_real * coherency_real + coherency_imaginary * coherency_imaginary
    gain_re, gain_im = (start_re, start_im)
    for repeat in range(SWEEPS):
        lift_re = fringe_real * gain_re.T[:, :, None] - fringe_imaginary * gain_im.T[:, :, None]
        lift_im = fringe_real * gain_im.T[:, :, None] + fringe_imaginary * gain_re.T[:, :, None]
        flat_re = lift_re.reshape(stations, groups * sources)
        flat_im = lift_im.reshape(stations, groups * sources)
        hold_re = (jnp.dot(res_re, flat_re, precision=highest_degree) - jnp.dot(res_im, flat_im, precision=highest_degree)).reshape(stations, groups, sources)
        hold_im = (jnp.dot(res_re, flat_im, precision=highest_degree) + jnp.dot(res_im, flat_re, precision=highest_degree)).reshape(stations, groups, sources)
        data_re = lax.optimization_barrier(jnp.sum(weighted_real * hold_re + weighted_imaginary * hold_im, axis=2)).T
        data_im = lax.optimization_barrier(jnp.sum(weighted_real * hold_im - weighted_imaginary * hold_re, axis=2)).T
        mix_re = start_re * gain_re + start_im * gain_im
        mix_im = start_re * gain_im - start_im * gain_re
        totals = jnp.einsum('kpq,ckq->ckp', power_map, jnp.stack([mix_re, mix_im, gain_re * gain_re + gain_im * gain_im]), precision=highest_degree)
        own_re = start_re * totals[0] - start_im * totals[1]
        own_im = start_re * totals[1] + start_im * totals[0]
        denominator = totals[2] + weight[:, None]
        gain_re = (data_re + own_re + weight[:, None] * goal_re) / denominator
        gain_im = (data_im + own_im + weight[:, None] * goal_im) / denominator
    return (gain_re, gain_im)

def shrink(columns, harmonics, cutoff):
    coeffs = jnp.einsum('km,cki->cmi', harmonics, columns, precision=highest_degree)
    magnitude = jnp.sqrt(coeffs[0] * coeffs[0] + coeffs[1] * coeffs[1])
    factor = jnp.maximum(magnitude - cutoff, 0.0) / jnp.maximum(magnitude, cutoff)
    return jnp.einsum('km,cmi->cki', harmonics, coeffs * factor[None], precision=highest_degree)

def reference(visibilities, station_uv, source_lm, source_flux, band_offset, gains_init, duals_init, poly_init, penalty, harmonics, threshold):
    legendre_all = legendre(band_offset)
    inverse = gram_inverse(band_offset)
    poly_shaped = poly_init.reshape(2, K, S, NTERM)

    def one_channel(chan_index):
        band_value = band_offset[chan_index]
        legendre_at = legendre(band_value)
        fringe_real, fringe_imaginary = phases(station_uv, source_lm, band_value)
        start = gains_init[:, :, chan_index, :]
        dual_now = duals_init[:, :, chan_index, :]
        field_re = (fringe_real * start[0].T[:, :, None] - fringe_imaginary * start[1].T[:, :, None]).reshape(S, K * NSRC)
        field_im = (fringe_real * start[1].T[:, :, None] + fringe_imaginary * start[0].T[:, :, None]).reshape(S, K * NSRC)
        flat_flux = source_flux.reshape(-1)
        model_re = jnp.dot(field_re * flat_flux, field_re.T, precision=highest_degree) + jnp.dot(field_im * flat_flux, field_im.T, precision=highest_degree)
        model_im = jnp.dot(field_im * flat_flux, field_re.T, precision=highest_degree) - jnp.dot(field_re * flat_flux, field_im.T, precision=highest_degree)
        res_re = visibilities[chan_index, :, 0, :] - model_re
        res_im = visibilities[chan_index, :, 1, :] - model_im
        target = lax.optimization_barrier(jnp.sum(poly_shaped * legendre_at, axis=3)) - dual_now / penalty[None, :, None]

        def one_cluster(cluster_index):
            gain_re, gain_im = refine(res_re, res_im, lax.dynamic_slice_in_dim(fringe_real, cluster_index, 1, 1), lax.dynamic_slice_in_dim(fringe_imaginary, cluster_index, 1, 1), lax.dynamic_slice_in_dim(source_flux, cluster_index, 1, 0), lax.dynamic_slice_in_dim(start[0], cluster_index, 1, 0), lax.dynamic_slice_in_dim(start[1], cluster_index, 1, 0), lax.dynamic_slice_in_dim(target[0], cluster_index, 1, 0), lax.dynamic_slice_in_dim(target[1], cluster_index, 1, 0), lax.dynamic_slice_in_dim(penalty, cluster_index, 1, 0))
            return jnp.stack([gain_re[0], gain_im[0]])
        solved = lax.map(one_cluster, jnp.arange(K).astype(jnp.int32))
        return jnp.transpose(solved, (1, 0, 2))
    solved_all = lax.map(one_channel, jnp.arange(NCH).astype(jnp.int32))
    gains_new = jnp.transpose(solved_all, (1, 2, 0, 3))
    spread = gains_new + duals_init / penalty[None, :, None, None]
    moments = jnp.einsum('ckfp,tf->ckpt', spread, legendre_all, precision=highest_degree)
    settled = jnp.einsum('ckpt,ut->ckpu', moments, inverse, precision=highest_degree).reshape(2, K, S * NTERM)
    consensus = shrink(settled, harmonics, threshold[0])
    fitted = jnp.einsum('ckpt,tf->ckfp', consensus.reshape(2, K, S, NTERM), legendre_all, precision=highest_degree)
    duals_new = duals_init + penalty[None, :, None, None] * (gains_new - fitted)
    return (gains_new, duals_new, consensus)
```

```python
import functools

import jax
import jax.numpy as jnp
import numpy as np
from jax import lax
from jax.experimental import pallas as pl
from jax.experimental.pallas import tpu as pltpu
from jax.sharding import PartitionSpec as P

NTERM = 4
MESH = pl.DeviceIdType.MESH
VM = pl.BlockSpec(memory_space=pltpu.VMEM)
ANY = pl.BlockSpec(memory_space=pltpu.HBM)
f32, bf16 = jnp.float32, jnp.bfloat16


def fit_half_circle():
    nodes = np.cos(np.pi * (np.arange(400) + 0.5) / 800.0) * 0.5
    square = nodes * nodes
    fit = np.polynomial.chebyshev.Chebyshev.fit
    root = np.sqrt(2.0)
    sine = fit(square, root * np.sin(np.pi * nodes) / nodes, 3, domain=[0, 0.25], w=nodes)
    cosine = fit(square, root * np.cos(np.pi * nodes), 4, domain=[0, 0.25])
    kind = np.polynomial.Polynomial
    return [[float(c) for c in p.convert(kind=kind).coef] for p in (sine, cosine)]


SINE, COSINE = fit_half_circle()


def horner(coefs, x):
    total = coefs[-1] * x + coefs[-2]
    for c in coefs[-3::-1]:
        total = total * x + c
    return total


def legendre(x):
    return [
        jnp.ones_like(x),
        x,
        0.5 * (3.0 * x * x - 1.0),
        0.5 * (5.0 * x * x * x - 3.0 * x),
    ]


def split(x):
    high = x.astype(bf16)
    low = (x - high.astype(f32)).astype(bf16)
    return high, low


def dot(a, b):
    return jnp.dot(a, b, preferred_element_type=f32)


def tdot(a, b):
    return lax.dot_general(a, b, (((0,), (0,)), ((), ())), preferred_element_type=f32)


def column(pen):
    count = pen.shape[1]
    row = lax.broadcasted_iota(jnp.int32, (count, count), 0)
    col = lax.broadcasted_iota(jnp.int32, (count, count), 1)
    return jnp.sum(jnp.where(row == col, pen[...], 0.0), axis=1, keepdims=True)


def halves(ref, rows):
    return jnp.concatenate([ref[pl.ds(j, rows, 2), :] for j in range(2)], axis=1)


def fit_taps(values):
    gram = [
        [jnp.sum(values[t] * values[s], axis=0, keepdims=True) for s in range(t + 1)]
        for t in range(NTERM)
    ]
    factor = [[None] * NTERM for _ in range(NTERM)]
    for t in range(NTERM):
        for s in range(t + 1):
            rest = gram[t][s]
            for r in range(s):
                rest = rest - factor[t][r] * factor[s][r]
            factor[t][s] = jnp.sqrt(rest) if s == t else rest / factor[s][s]
    half = []
    for t in range(NTERM):
        rest = values[t]
        for s in range(t):
            rest = rest - factor[t][s] * half[s]
        half.append(rest / factor[t][t])
    taps = [None] * NTERM
    for t in reversed(range(NTERM)):
        rest = half[t]
        for s in range(t + 1, NTERM):
            rest = rest - factor[s][t] * taps[s]
        taps[t] = rest / factor[t][t]
    return taps


def step_kernel(
    n_dir, n_chan, group,
    vis_hbm, uv, lm, flux, band, g_ref, dual_hbm, poly_hbm, pen_ref, harm_hbm, cut,
    gains_out, blocks,
    vis, dual, poly, harm,
    b_ref, b_all, pack, src, g, er, ei,
    erh, erl, eih, eil, nih, nil,
    frh, frl, fih, fil, drh, drl, srh, srl,
    partial, partner,
    rs, y, n, power, xs, tcol, goal, offset, hm,
    packed, zin, own, zall, part, gains,
    ins, gs, gr, ms, mr, bs, br, s1, r1, s2, r2, s3, r3, outs,
):
    rows2, stations = g.shape
    clusters = rows2 // 2
    sources = er.shape[0] // clusters
    flat = clusters * sources
    me_d, me_c = lax.axis_index("dir"), lax.axis_index("chan")
    barrier = pltpu.get_barrier_semaphore()
    for j in range(1, n_dir):
        pl.semaphore_signal(
            barrier, inc=1, device_id={"dir": lax.rem(me_d + j, n_dir)}, device_id_type=MESH
        )
    for j in range(1, n_chan):
        pl.semaphore_signal(
            barrier, inc=1, device_id={"chan": lax.rem(me_c + j, n_chan)}, device_id_type=MESH
        )
    loads = [
        pltpu.make_async_copy(a, b, ins.at[i])
        for i, (a, b) in enumerate(
            [(vis_hbm, vis), (dual_hbm, dual), (poly_hbm, poly), (harm_hbm, harm)]
        )
    ]
    for c in loads:
        c.start()

    def send(s, d, a, b, peer):
        return pltpu.make_async_remote_copy(
            src_ref=s, dst_ref=d, send_sem=a, recv_sem=b, device_id=peer, device_id_type=MESH
        )

    table = jnp.concatenate([lm[0], lm[1], jnp.sqrt(flux[...])], axis=0)
    fill = (-3 * clusters) % 128
    table = jnp.concatenate([table, jnp.zeros((fill, sources), f32)], axis=0)
    pack[0, : 4 * clusters, :] = g_ref[...]
    pack[0, 4 * clusters : 4 * clusters + sources, :] = jnp.transpose(table)
    here = band[...]
    b_ref[...] = jnp.broadcast_to(here, b_ref.shape)
    b_all[0] = b_ref[...]
    stretch = 1.0 + 0.25 * here
    u = uv[0:1, :] * stretch
    v = uv[1:2, :] * stretch

    def open_pack(slot):
        g_all = halves(pack.at[slot, : 4 * clusters], rows2)
        g[...] = g_all
        t = pack[slot, 4 * clusters : 4 * clusters + sources, :]
        for k in range(clusters):
            src[k * sources : (k + 1) * sources, :] = pltpu.roll(t, (128 - k) % 128, 1)
        return g_all

    chunk = 4
    span = chunk * sources

    def circle(start):
        cols = src[pl.ds(start, span), :]
        turns = cols[:, 0:1] * u + cols[:, clusters : clusters + 1] * v
        r = turns - jnp.round(turns)
        square = r * r
        s = r * horner(SINE, square)
        c = horner(COSINE, square)
        w = cols[:, 2 * clusters : 2 * clusters + 1]
        ws = w * s
        return w - ws * s, ws * c

    def times(e_r, e_i, c, ref):
        f_r, f_i = [], []
        for i in range(chunk):
            a = ref[pl.ds(c * chunk + i, 1), :]
            b = ref[pl.ds(clusters + c * chunk + i, 1), :]
            p_r = e_r[i * sources : (i + 1) * sources]
            p_i = e_i[i * sources : (i + 1) * sources]
            f_r.append(p_r * a - p_i * b)
            f_i.append(p_r * b + p_i * a)
        return jnp.concatenate(f_r, axis=0), jnp.concatenate(f_i, axis=0)

    def put(h_ref, l_ref, start, x):
        h, l = split(x)
        h_ref[pl.ds(start, span), :] = h
        l_ref[pl.ds(start, span), :] = l
        return h, l

    def fields(keep):
        def body(c, carry):
            start = pl.multiple_of(c * span, span)
            e_r, e_i = circle(start)
            if keep:
                er[pl.ds(start, span), :] = e_r
                ei[pl.ds(start, span), :] = e_i
                put(erh, erl, start, e_r)
                h, l = put(eih, eil, start, e_i)
                nih[pl.ds(start, span), :] = -h
                nil[pl.ds(start, span), :] = -l
            f_r, f_i = times(e_r, e_i, c, g)
            off = 0 if keep else flat
            put(frh, frl, start + off, f_r)
            put(fih, fil, start + off, f_i)
            put(drh, drl, start, f_r - f_i)
            put(srh, srl, start, f_i + f_r)
            return carry

        lax.fori_loop(0, clusters // chunk, body, 0)

    def model(off):
        def rows(a, b):
            return jnp.concatenate([a[off : off + flat, :], b[off : off + flat, :]], axis=0)

        d_h = jnp.concatenate([drh[...], srh[...]], axis=0)
        d_l = jnp.concatenate([drl[...], srl[...]], axis=0)
        first = tdot(rows(frh, fih), jnp.concatenate([d_h, d_l], axis=1))
        second = tdot(rows(frl, fil), d_h)
        return first[:, :stations] + first[:, stations:] + second

    g_own = open_pack(0)
    g_r, g_i = g_own[:clusters], g_own[clusters:]
    fields(True)

    pl.semaphore_wait(barrier, n_dir + n_chan - 2)
    per = n_dir // group
    gathers = []
    for j in range(1, per):
        peer = {"dir": lax.rem(me_d + n_dir - group * j, n_dir)}
        gathers.append(send(pack.at[0], pack.at[j], gs.at[j], gr.at[j], peer))
    bands = []
    for j in range(1, n_chan):
        peer = {"chan": lax.rem(me_c + n_chan - j, n_chan)}
        bands.append(send(b_ref, b_all.at[j], bs.at[j], br.at[j], peer))
    for c in gathers + bands:
        c.start()

    partial[...] = model(0)

    def others(j, carry):
        for i in range(1, per):

            @pl.when(j == i)
            def _():
                gathers[i - 1].wait_recv()

        open_pack(j)
        fields(False)
        partial[...] += model(flat)
        return carry

    lax.fori_loop(1, per, others, 0)
    if group == 2:
        mate = {"dir": me_d + 1 - 2 * lax.rem(me_d, 2)}
        swap = send(partial, partner, ms.at[0], mr.at[0], mate)
        swap.start()

    xs[:clusters, :] = g_r * g_r + g_i * g_i
    lane = lax.broadcasted_iota(jnp.int32, (stations, 128), 1)
    tcol[...] = jnp.zeros((stations, 128), f32)

    def powers(k, carry):
        at = pl.ds(pl.multiple_of(k * sources, sources), sources)
        r_h, r_l, i_h, i_l = erh[at, :], erl[at, :], eih[at, :], eil[at, :]
        n_h, n_l = nih[at, :], nil[at, :]
        left = jnp.concatenate([r_h, i_h, r_h, i_h, r_l, i_l], axis=0)
        real = jnp.concatenate([r_h, i_h, r_l, i_l, r_h, i_h], axis=0)
        imag = jnp.concatenate([n_h, r_h, n_l, r_l, n_h, r_h], axis=0)
        c = tdot(left, jnp.concatenate([real, imag], axis=1))
        c_r, c_i = c[:, :stations], c[:, stations:]
        w = c_r * c_r + c_i * c_i
        power[k] = w
        t = jnp.sum(w * xs[pl.ds(k, 1), :], axis=1, keepdims=True)
        tcol[...] = jnp.where(lane == k, t, tcol[...])
        return carry

    lax.fori_loop(0, clusters, powers, 0)

    for c in loads[1:]:
        c.wait()
    level = legendre(here)
    pen = column(pen_ref)
    pull = jnp.concatenate([pen, pen], axis=0)
    tile = 32 * NTERM
    tiles = stations // 32
    row = lax.broadcasted_iota(jnp.int32, (tile, tile), 0)
    col = lax.broadcasted_iota(jnp.int32, (tile, tile), 1)
    pick = jnp.zeros((tile, tile), f32)
    for t in range(NTERM):
        pick = jnp.where(row - NTERM * col == t, level[t], pick)
    p_h, p_l = split(pick)
    q_h, q_l = split(
        jnp.concatenate([poly[:, j * tile : (j + 1) * tile] for j in range(tiles)], axis=0)
    )
    value = dot(
        jnp.concatenate([q_h, q_l, q_h], axis=1), jnp.concatenate([p_h, p_h, p_l], axis=0)
    )
    value = jnp.concatenate(
        [value[j * rows2 : (j + 1) * rows2, :32] for j in range(tiles)], axis=1
    )
    offset[...] = halves(dual, rows2) / pull
    goal[...] = (value - offset[...]) * pull
    modes = harm.shape[1]
    mode_rows = hm.shape[0]
    turned = jnp.concatenate(
        [harm[...], jnp.zeros((harm.shape[0], mode_rows - modes), f32)], axis=1
    )
    h_h, h_l = split(jnp.transpose(turned))
    hm[...] = jnp.concatenate([h_h, h_h, h_l], axis=1)
    for c in bands:
        c.wait()
    taps = fit_taps(legendre(b_all[:, 0, :]))

    loads[0].wait()
    if group == 2:
        swap.wait()
        both = partial[...] + partner[...]
    else:
        both = partial[...]
    turned = jnp.transpose(both)

    def seen(i):
        return jnp.concatenate(
            [vis[pl.ds(2 * j + i, stations, 4), :] for j in range(2)], axis=1
        )

    r_h, r_l = split(seen(0) - 0.5 * (both + turned))
    i_h, i_l = split(seen(1) - 0.5 * (both - turned))
    rs[0, :, :stations] = r_h
    rs[0, :, stations:] = -i_h
    rs[1, :, :stations] = i_h
    rs[1, :, stations:] = r_h
    rs[2, :, :stations] = r_l
    rs[2, :, stations:] = -i_l
    rs[3, :, :stations] = i_l
    rs[3, :, stations:] = r_l

    def gather_rows():
        a, b = frh[:flat, :], fih[:flat, :]
        y[...] = dot(
            jnp.concatenate([a, b, a, b, frl[:flat, :], fil[:flat, :]], axis=1),
            jnp.concatenate([rs[0], rs[1], rs[2], rs[3], rs[0], rs[1]], axis=0),
        )

        def body(k, carry):
            at = pl.ds(pl.multiple_of(k * sources, sources), sources)
            e_r, e_i = er[at, :], ei[at, :]
            y_r, y_i = y[at, :stations], y[at, stations:]
            n[pl.ds(k, 1), :] = jnp.sum(e_r * y_r + e_i * y_i, axis=0, keepdims=True)
            n[pl.ds(clusters + k, 1), :] = jnp.sum(e_r * y_i - e_i * y_r, axis=0, keepdims=True)
            return carry

        lax.fori_loop(0, clusters, body, 0)

    gather_rows()
    total = jnp.transpose(tcol[...])[:clusters]
    inverse = 1.0 / (total + pen)
    h_r = (n[:clusters, :] + g_r * total + goal[:clusters, :]) * inverse
    h_i = (n[clusters:, :] + g_i * total + goal[clusters:, :]) * inverse
    xs[:clusters, :] = g_r * h_r + g_i * h_i
    xs[clusters:rows2, :] = g_r * h_i - g_i * h_r
    xs[rows2:, :] = h_r * h_r + h_i * h_i
    g[:clusters, :] = h_r
    g[clusters:, :] = h_i

    def again(c, carry):
        start = pl.multiple_of(c * span, span)
        at = pl.ds(start, span)
        f_r, f_i = times(er[at, :], ei[at, :], c, g)
        put(frh, frl, start, f_r)
        put(fih, fil, start, f_i)
        return carry

    lax.fori_loop(0, clusters // chunk, again, 0)
    gather_rows()

    def totals(k, carry):
        w = power[k]
        acc = tcol[...]
        for i in range(3):
            t = jnp.sum(w * xs[pl.ds(i * clusters + k, 1), :], axis=1, keepdims=True)
            acc = jnp.where(lane == i * clusters + k, t, acc)
        tcol[...] = acc
        return carry

    lax.fori_loop(0, clusters, totals, 0)
    sums = jnp.transpose(tcol[...])
    t_0, t_1, t_2 = (sums[i * clusters : (i + 1) * clusters] for i in range(3))
    inverse = 1.0 / (t_2 + pen)
    new_r = (n[:clusters, :] + g_r * t_0 - g_i * t_1 + goal[:clusters, :]) * inverse
    new_i = (n[clusters:, :] + g_r * t_1 + g_i * t_0 + goal[clusters:, :]) * inverse
    new = jnp.concatenate([new_r, new_i], axis=0)
    gains[...] = new
    emit = pltpu.make_async_copy(gains, gains_out, outs.at[0])
    emit.start()

    spread = new + offset[...]
    each = stations // n_chan
    groups = rows2 // 8
    used = groups * each
    lanes = packed.shape[2]
    for j in range(n_chan):
        if used < lanes:
            packed[j] = jnp.zeros((8, lanes), f32)
        packed[j, :, :used] = jnp.concatenate(
            [spread[8 * i : 8 * i + 8, j * each : (j + 1) * each] for i in range(groups)], axis=1
        )
    first = []
    for j in range(1, n_chan):
        peer = lax.rem(me_c + n_chan - j, n_chan)
        first.append(send(packed.at[peer], zin.at[j], s1.at[j], r1.at[j], {"chan": peer}))
    for c in first:
        c.start()
    mixed = [packed[me_c] * taps[t][0:1, 0:1] for t in range(NTERM)]
    for j in range(1, n_chan):
        first[j - 1].wait_recv()
        got = zin[j]
        for t in range(NTERM):
            mixed[t] = mixed[t] + got * taps[t][j : j + 1, 0:1]
    wide = NTERM * each
    width = own.shape[1]
    if wide < width:
        own[...] = jnp.zeros_like(own)
    for i in range(groups):
        own[8 * i : 8 * i + 8, :wide] = jnp.concatenate(
            [mixed[t][:, i * each : (i + 1) * each] for t in range(NTERM)], axis=1
        )
    second = []
    for j in range(1, n_dir):
        peer = lax.rem(me_d + j, n_dir)
        second.append(send(own, zall.at[me_d], s2.at[j], r2.at[j], {"dir": peer}))
    for c in second:
        c.start()
    zall[me_d] = own[...]
    for c in second:
        c.wait()
    z_h, z_l = split(
        jnp.concatenate(
            [
                jnp.concatenate([zall[d][:clusters], zall[d][clusters:]], axis=1)
                for d in range(n_dir)
            ],
            axis=0,
        )
    )
    a = dot(hm[...], jnp.concatenate([z_h, z_l, z_h], axis=0))
    a_r, a_i = a[:, :width], a[:, width:]
    size = jnp.sqrt(a_r * a_r + a_i * a_i)
    limit = cut[...]
    scale = jnp.maximum(size - limit, 0.0) / jnp.maximum(size, limit)
    a_h, a_l = split(jnp.concatenate([a_r * scale, a_i * scale], axis=1)[:modes])
    m_h, m_l = split(harm[pl.ds(pl.multiple_of(me_d * clusters, clusters), clusters), :])
    twice = dot(jnp.concatenate([m_h, m_l], axis=0), a_h)
    done = twice[:clusters] + twice[clusters:] + dot(m_h, a_l)
    part[:clusters] = done[:, :width]
    part[clusters:] = done[:, width:]
    third = []
    for j in range(1, n_chan):
        peer = lax.rem(me_c + j, n_chan)
        third.append(send(part, blocks.at[me_c], s3.at[j], r3.at[j], {"chan": peer}))
    for c in third:
        c.start()
    keep = pltpu.make_async_copy(part, blocks.at[me_c], outs.at[1])
    keep.start()
    for c in gathers + first:
        c.wait_send()
    emit.wait()
    keep.wait()
    for c in third:
        c.wait()


def emit_kernel(blocks, gains, dual, pen_ref, band, gains_out, dual_out, cons_out):
    n_chan, rows2, width = blocks.shape
    stations = gains.shape[1]
    each = stations // n_chan
    wide = NTERM * each
    level = legendre(band[...])
    row = lax.broadcasted_iota(jnp.int32, (width, width), 0)
    col = lax.broadcasted_iota(jnp.int32, (width, width), 1)
    weave = jnp.zeros((width, width), f32)
    sample = jnp.zeros((width, width), f32)
    for t in range(NTERM):
        place = row - t * each
        inside = (place >= 0) & (place < each)
        weave = jnp.where(inside & (col == NTERM * place + t), 1.0, weave)
        sample = jnp.where(inside & (col == place), level[t], sample)
    s_h, s_l = split(sample)
    both = jnp.concatenate([weave.astype(bf16), s_h], axis=1)
    rest = jnp.concatenate([jnp.zeros((width, width), bf16), s_l], axis=1)
    b_h, b_l = split(jnp.concatenate([blocks[j] for j in range(n_chan)], axis=0))
    result = dot(
        jnp.concatenate([b_h, b_l, b_h], axis=1), jnp.concatenate([both, both, rest], axis=0)
    )
    fitted = []
    for j in range(n_chan):
        piece = result[j * rows2 : (j + 1) * rows2]
        cons_out[:, j * wide : (j + 1) * wide] = piece[:, :wide]
        fitted.append(piece[:, width : width + each])
    fitted = jnp.concatenate(fitted, axis=1)
    pen = column(pen_ref)
    pull = jnp.concatenate([pen, pen], axis=0)
    new = gains[...]
    fresh = halves(dual, rows2) + pull * (new - fitted)
    for j in range(2):
        gains_out[pl.ds(j, rows2, 2), :] = new[:, j * 128 : (j + 1) * 128]
        dual_out[pl.ds(j, rows2, 2), :] = fresh[:, j * 128 : (j + 1) * 128]


def solution(mesh):
    n_dir, n_chan = mesh.shape["dir"], mesh.shape["chan"]
    group = 2 if n_dir % 2 == 0 else 1

    def shards(
        visibilities, station_uv, source_lm, source_flux, band_offset, gains_init, duals_init,
        poly_init, penalty, harmonics, threshold,
    ):
        _, clusters, sources = source_lm.shape
        stations = station_uv.shape[1]
        modes = harmonics.shape[1]
        mode_rows = -(-modes // 128) * 128
        rows2 = 2 * clusters
        lanes = max(128, stations * NTERM // n_chan)
        flat = clusters * sources
        small = max(128, stations // n_chan * (rows2 // 8))
        vis = visibilities.reshape(stations, 2, stations // 128, 128)
        vis = vis.transpose(0, 2, 1, 3).reshape(stations * 4, 128)
        lines = rows2 * stations // 128
        dual = duals_init.reshape(lines, 128)
        band = band_offset.reshape(1, 1)
        pen = penalty.reshape(1, clusters)
        dma = pltpu.SemaphoreType.DMA
        vm = pltpu.VMEM
        wide16 = vm((flat, stations), bf16)
        long16 = vm((2 * flat, stations), bf16)
        per = n_dir // group
        gains, blocks = pl.pallas_call(
            functools.partial(step_kernel, n_dir, n_chan, group),
            out_shape=(
                jax.ShapeDtypeStruct((rows2, stations), f32),
                jax.ShapeDtypeStruct((n_chan, rows2, lanes), f32),
            ),
            in_specs=[ANY, VM, VM, VM, VM, VM, ANY, ANY, VM, ANY, VM],
            out_specs=(ANY, ANY),
            scratch_shapes=[
                vm((stations * 4, 128), f32),
                vm((lines, 128), f32),
                vm((rows2, stations * NTERM), f32),
                vm(harmonics.shape, f32),
                vm((8, 128), f32),
                vm((n_chan, 8, 128), f32),
                vm((per, lines + sources, 128), f32),
                vm((flat, 128), f32),
                vm((rows2, stations), f32),
                vm((flat, stations), f32),
                vm((flat, stations), f32),
                wide16, wide16, wide16, wide16, wide16, wide16,
                long16, long16, long16, long16,
                wide16, wide16, wide16, wide16,
                vm((stations, stations), f32),
                vm((stations, stations), f32),
                vm((4, stations, 2 * stations), bf16),
                vm((flat, 2 * stations), f32),
                vm((rows2, stations), f32),
                vm((clusters, stations, stations), f32),
                vm((3 * clusters, stations), f32),
                vm((stations, 128), f32),
                vm((rows2, stations), f32),
                vm((rows2, stations), f32),
                vm((mode_rows, 3 * harmonics.shape[0]), bf16),
                vm((n_chan, 8, small), f32),
                vm((n_chan, 8, small), f32),
                vm((rows2, lanes), f32),
                vm((n_dir, rows2, lanes), f32),
                vm((rows2, lanes), f32),
                vm((rows2, stations), f32),
                dma((4,)),
                dma((per,)), dma((per,)),
                dma((1,)), dma((1,)),
                dma((n_chan,)), dma((n_chan,)),
                dma((n_chan,)), dma((n_chan,)),
                dma((n_dir,)), dma((n_dir,)),
                dma((n_chan,)), dma((n_chan,)),
                dma((2,)),
            ],
            compiler_params=pltpu.CompilerParams(
                collective_id=0, has_side_effects=True, vmem_limit_bytes=62 * 2**20
            ),
            name="calibrate",
        )(
            vis, station_uv, source_lm, source_flux, band, gains_init.reshape(lines, 128), dual,
            poly_init.reshape(rows2, stations * NTERM), pen, harmonics, threshold.reshape(1, 1),
        )
        gains, duals, consensus = pl.pallas_call(
            emit_kernel,
            out_shape=(
                jax.ShapeDtypeStruct((lines, 128), f32),
                jax.ShapeDtypeStruct((lines, 128), f32),
                jax.ShapeDtypeStruct((rows2, stations * NTERM), f32),
            ),
            in_specs=[VM] * 5,
            out_specs=(VM,) * 3,
            name="emit",
        )(blocks, gains, dual, pen, band)
        shape = (2, clusters, 1, stations)
        return (
            gains.reshape(shape),
            duals.reshape(shape),
            consensus.reshape(2, clusters, stations * NTERM),
        )

    return jax.shard_map(
        shards,
        mesh=mesh,
        in_specs=(
            P("chan", None, None, None),
            P(),
            P(None, "dir", None),
            P("dir", None),
            P("chan"),
            P(None, "dir", "chan", None),
            P(None, "dir", "chan", None),
            P(None, "dir", None),
            P("dir"),
            P(),
            P(),
        ),
        out_specs=(
            P(None, "dir", "chan", None),
            P(None, "dir", "chan", None),
            P(None, "dir", None),
        ),
        check_vma=False,
    )
```

```python
import functools

import jax
import jax.numpy as jnp
import numpy as np
from jax import lax
from jax.experimental import pallas as pl
from jax.experimental.pallas import tpu as pltpu
from jax.sharding import PartitionSpec as P

NTERM = 4
MESH = pl.DeviceIdType.MESH
VM = pl.BlockSpec(memory_space=pltpu.VMEM)
ANY = pl.BlockSpec(memory_space=pltpu.HBM)
f32, bf16 = jnp.float32, jnp.bfloat16


def fit_half_circle():
    nodes = np.cos(np.pi * (np.arange(400) + 0.5) / 800.0) * 0.5
    square = nodes * nodes
    fit = np.polynomial.chebyshev.Chebyshev.fit
    root = np.sqrt(2.0)
    sine = fit(square, root * np.sin(np.pi * nodes) / nodes, 3, domain=[0, 0.25], w=nodes)
    cosine = fit(square, root * np.cos(np.pi * nodes), 4, domain=[0, 0.25])
    kind = np.polynomial.Polynomial
    return [[float(c) for c in p.convert(kind=kind).coef] for p in (sine, cosine)]


SINE, COSINE = fit_half_circle()


def horner(coefs, x):
    total = coefs[-1] * x + coefs[-2]
    for c in coefs[-3::-1]:
        total = total * x + c
    return total


def legendre(x):
    return [
        jnp.ones_like(x),
        x,
        0.5 * (3.0 * x * x - 1.0),
        0.5 * (5.0 * x * x * x - 3.0 * x),
    ]


def split(x):
    high = x.astype(bf16)
    low = (x - high.astype(f32)).astype(bf16)
    return high, low


def dot(a, b):
    return jnp.dot(a, b, preferred_element_type=f32)


def tdot(a, b):
    return lax.dot_general(a, b, (((0,), (0,)), ((), ())), preferred_element_type=f32)


def column(pen):
    count = pen.shape[1]
    row = lax.broadcasted_iota(jnp.int32, (count, count), 0)
    col = lax.broadcasted_iota(jnp.int32, (count, count), 1)
    return jnp.sum(jnp.where(row == col, pen[...], 0.0), axis=1, keepdims=True)


def halves(ref, rows):
    return jnp.concatenate([ref[pl.ds(j, rows, 2), :] for j in range(2)], axis=1)


def fit_taps(values):
    gram = [
        [jnp.sum(values[t] * values[s], axis=0, keepdims=True) for s in range(t + 1)]
        for t in range(NTERM)
    ]
    factor = [[None] * NTERM for _ in range(NTERM)]
    for t in range(NTERM):
        for s in range(t + 1):
            rest = gram[t][s]
            for r in range(s):
                rest = rest - factor[t][r] * factor[s][r]
            factor[t][s] = jnp.sqrt(rest) if s == t else rest / factor[s][s]
    half = []
    for t in range(NTERM):
        rest = values[t]
        for s in range(t):
            rest = rest - factor[t][s] * half[s]
        half.append(rest / factor[t][t])
    taps = [None] * NTERM
    for t in reversed(range(NTERM)):
        rest = half[t]
        for s in range(t + 1, NTERM):
            rest = rest - factor[s][t] * taps[s]
        taps[t] = rest / factor[t][t]
    return taps


def step_kernel(
    n_dir, n_chan, group,
    vis_hbm, uv_hbm, lm_hbm, flux_hbm, band_hbm, g_hbm, dual_hbm, poly_hbm, pen_hbm, harm_hbm,
    cut_hbm,
    gains_out, blocks, band_out,
    vis, uv, lm, flux, band, dual, poly, pen_ref, harm, cut,
    b_ref, b_all, pack, src, g, er, ei,
    erh, erl, eih, eil, nih, nil,
    frh, frl, fih, fil, drh, drl, srh, srl,
    partial, partner,
    rs, power, xs, sums, tcol, goal, offset, hm,
    packed, zin, own, zall, part, gains,
    ins, gs, gr, ms, mr, bs, br, s1, r1, s2, r2, s3, r3, outs,
):
    rows2, stations = g.shape
    clusters = rows2 // 2
    sources = er.shape[0] // clusters
    flat = clusters * sources
    me_d, me_c = lax.axis_index("dir"), lax.axis_index("chan")
    barrier = pltpu.get_barrier_semaphore()
    for j in range(1, n_dir):
        pl.semaphore_signal(
            barrier, inc=1, device_id={"dir": lax.rem(me_d + j, n_dir)}, device_id_type=MESH
        )
    for j in range(1, n_chan):
        pl.semaphore_signal(
            barrier, inc=1, device_id={"chan": lax.rem(me_c + j, n_chan)}, device_id_type=MESH
        )
    loads = [
        pltpu.make_async_copy(a, b, ins.at[i])
        for i, (a, b) in enumerate(
            [
                (band_hbm, band),
                (lm_hbm, lm),
                (flux_hbm, flux),
                (g_hbm, pack.at[0, : 4 * clusters]),
                (uv_hbm, uv),
                (cut_hbm, cut),
                (dual_hbm, dual),
                (poly_hbm, poly),
                (pen_hbm, pen_ref),
                (harm_hbm, harm),
                (vis_hbm, vis),
            ]
        )
    ]
    for c in loads:
        c.start()

    def send(s, d, a, b, peer):
        return pltpu.make_async_remote_copy(
            src_ref=s, dst_ref=d, send_sem=a, recv_sem=b, device_id=peer, device_id_type=MESH
        )

    for c in loads[:5]:
        c.wait()
    table = jnp.concatenate([lm[0], lm[1], jnp.sqrt(flux[...])], axis=0)
    fill = (-3 * clusters) % 128
    table = jnp.concatenate([table, jnp.zeros((fill, sources), f32)], axis=0)
    pack[0, 4 * clusters : 4 * clusters + sources, :] = jnp.transpose(table)
    here = jnp.full((1, 1), band[0], f32)
    b_ref[...] = jnp.full(b_ref.shape, band[0], f32)
    b_all[0] = b_ref[...]
    stretch = 1.0 + 0.25 * here
    u = uv[0:1, :] * stretch
    v = uv[1:2, :] * stretch

    def open_pack(slot):
        g_all = halves(pack.at[slot, : 4 * clusters], rows2)
        g[...] = g_all
        t = pack[slot, 4 * clusters : 4 * clusters + sources, :]
        for k in range(clusters):
            src[k * sources : (k + 1) * sources, :] = pltpu.roll(t, (128 - k) % 128, 1)
        return g_all

    chunk = 4
    span = chunk * sources

    def circle(start):
        cols = src[pl.ds(start, span), :]
        turns = cols[:, 0:1] * u + cols[:, clusters : clusters + 1] * v
        r = turns - jnp.round(turns)
        square = r * r
        s = r * horner(SINE, square)
        c = horner(COSINE, square)
        w = cols[:, 2 * clusters : 2 * clusters + 1]
        ws = w * s
        return w - ws * s, ws * c

    def times(e_r, e_i, c, ref):
        f_r, f_i = [], []
        for i in range(chunk):
            a = ref[pl.ds(c * chunk + i, 1), :]
            b = ref[pl.ds(clusters + c * chunk + i, 1), :]
            p_r = e_r[i * sources : (i + 1) * sources]
            p_i = e_i[i * sources : (i + 1) * sources]
            f_r.append(p_r * a - p_i * b)
            f_i.append(p_r * b + p_i * a)
        return jnp.concatenate(f_r, axis=0), jnp.concatenate(f_i, axis=0)

    def put(h_ref, l_ref, start, x):
        h, l = split(x)
        h_ref[pl.ds(start, span), :] = h
        l_ref[pl.ds(start, span), :] = l
        return h, l

    def field_chunk(c, keep):
        start = pl.multiple_of(c * span, span)
        e_r, e_i = circle(start)
        if keep:
            er[pl.ds(start, span), :] = e_r
            ei[pl.ds(start, span), :] = e_i
            put(erh, erl, start, e_r)
            h, l = put(eih, eil, start, e_i)
            nih[pl.ds(start, span), :] = -h
            nil[pl.ds(start, span), :] = -l
        f_r, f_i = times(e_r, e_i, c, g)
        off = 0 if keep else flat
        put(frh, frl, start + off, f_r)
        put(fih, fil, start + off, f_i)
        put(drh, drl, start, f_r - f_i)
        put(srh, srl, start, f_i + f_r)

    lane = lax.broadcasted_iota(jnp.int32, (stations, 128), 1)

    def power_chunk(c):
        acc = tcol[...]
        for i in range(chunk):
            k = c * chunk + i
            at = pl.ds(pl.multiple_of(k * sources, sources), sources)
            r_h, r_l, i_h, i_l = erh[at, :], erl[at, :], eih[at, :], eil[at, :]
            n_h, n_l = nih[at, :], nil[at, :]
            left = jnp.concatenate([r_h, i_h, r_h, i_h, r_l, i_l], axis=0)
            real = jnp.concatenate([r_h, i_h, r_l, i_l, r_h, i_h], axis=0)
            imag = jnp.concatenate([n_h, r_h, n_l, r_l, n_h, r_h], axis=0)
            both = tdot(left, jnp.concatenate([real, imag], axis=1))
            c_r, c_i = both[:, :stations], both[:, stations:]
            w = c_r * c_r + c_i * c_i
            power[k] = w
            t = jnp.sum(w * xs[pl.ds(k, 1), :], axis=1, keepdims=True)
            acc = jnp.where(lane == k, t, acc)
        tcol[...] = acc

    def chunks(body):
        def step(c, carry):
            body(c)
            return carry

        lax.fori_loop(0, clusters // chunk, step, 0)

    def model(off):
        def rows(a, b):
            return jnp.concatenate([a[off : off + flat, :], b[off : off + flat, :]], axis=0)

        d_h = jnp.concatenate([drh[...], srh[...]], axis=0)
        d_l = jnp.concatenate([drl[...], srl[...]], axis=0)
        first = tdot(rows(frh, fih), jnp.concatenate([d_h, d_l], axis=1))
        second = tdot(rows(frl, fil), d_h)
        return first[:, :stations] + first[:, stations:] + second

    g_own = open_pack(0)
    g_r, g_i = g_own[:clusters], g_own[clusters:]
    xs[:clusters, :] = g_r * g_r + g_i * g_i
    tcol[...] = jnp.zeros((stations, 128), f32)
    chunks(lambda c: field_chunk(c, True))

    pl.semaphore_wait(barrier, n_dir + n_chan - 2)
    per = n_dir // group
    gathers = []
    for j in range(1, per):
        peer = {"dir": lax.rem(me_d + n_dir - group * j, n_dir)}
        gathers.append(send(pack.at[0], pack.at[j], gs.at[j], gr.at[j], peer))
    bands = []
    for j in range(1, n_chan):
        peer = {"chan": lax.rem(me_c + n_chan - j, n_chan)}
        bands.append(send(b_ref, b_all.at[j], bs.at[j], br.at[j], peer))
    for c in gathers + bands:
        c.start()

    partial[...] = model(0)

    def first_other(c):
        field_chunk(c, False)
        power_chunk(c)

    if per > 1:
        gathers[0].wait_recv()
        open_pack(1)
        chunks(first_other)
        partial[...] += model(flat)
    else:
        chunks(power_chunk)

    def others(j, carry):
        for i in range(2, per):

            @pl.when(j == i)
            def _():
                gathers[i - 1].wait_recv()

        open_pack(j)
        chunks(lambda c: field_chunk(c, False))
        partial[...] += model(flat)
        return carry

    if per > 2:
        lax.fori_loop(2, per, others, 0)
    if group == 2:
        mate = {"dir": me_d + 1 - 2 * lax.rem(me_d, 2)}
        swap = send(partial, partner, ms.at[0], mr.at[0], mate)
        swap.start()

    for c in loads[5:10]:
        c.wait()
    level = legendre(here)
    pen = column(pen_ref)
    pull = jnp.concatenate([pen, pen], axis=0)
    tile = 32 * NTERM
    tiles = stations // 32
    row = lax.broadcasted_iota(jnp.int32, (tile, tile), 0)
    col = lax.broadcasted_iota(jnp.int32, (tile, tile), 1)
    pick = jnp.zeros((tile, tile), f32)
    for t in range(NTERM):
        pick = jnp.where(row - NTERM * col == t, level[t], pick)
    p_h, p_l = split(pick)
    q_h, q_l = split(
        jnp.concatenate([poly[:, j * tile : (j + 1) * tile] for j in range(tiles)], axis=0)
    )
    value = dot(
        jnp.concatenate([q_h, q_l, q_h], axis=1), jnp.concatenate([p_h, p_h, p_l], axis=0)
    )
    value = jnp.concatenate(
        [value[j * rows2 : (j + 1) * rows2, :32] for j in range(tiles)], axis=1
    )
    offset[...] = halves(dual, rows2) / pull
    goal[...] = (value - offset[...]) * pull
    modes = harm.shape[1]
    mode_rows = hm.shape[0]
    turned = jnp.concatenate(
        [harm[...], jnp.zeros((harm.shape[0], mode_rows - modes), f32)], axis=1
    )
    h_h, h_l = split(jnp.transpose(turned))
    hm[...] = jnp.concatenate([h_h, h_h, h_l], axis=1)
    for c in bands:
        c.wait()
    taps = fit_taps(legendre(b_all[:, 0, :]))

    loads[10].wait()
    if group == 2:
        swap.wait()
        both = partial[...] + partner[...]
    else:
        both = partial[...]
    turned = jnp.transpose(both)

    def seen(i):
        return jnp.concatenate(
            [vis[pl.ds(2 * j + i, stations, 4), :] for j in range(2)], axis=1
        )

    r_h, r_l = split(seen(0) - 0.5 * (both + turned))
    i_h, i_l = split(seen(1) - 0.5 * (both - turned))
    rs[0, :, :stations] = r_h
    rs[0, :, stations:] = -i_h
    rs[1, :, :stations] = i_h
    rs[1, :, stations:] = r_h
    rs[2, :, :stations] = r_l
    rs[2, :, stations:] = -i_l
    rs[3, :, :stations] = i_l
    rs[3, :, stations:] = r_l

    def gather_rows():
        a, b = frh[:flat, :], fih[:flat, :]
        y = dot(
            jnp.concatenate([a, b, a, b, frl[:flat, :], fil[:flat, :]], axis=1),
            jnp.concatenate([rs[0], rs[1], rs[2], rs[3], rs[0], rs[1]], axis=0),
        )
        y_r, y_i = y[:, :stations], y[:, stations:]
        e_r, e_i = er[...], ei[...]

        def over(x):
            return jnp.sum(x.reshape(clusters, sources, stations), axis=1)

        return over(e_r * y_r + e_i * y_i), over(e_r * y_i - e_i * y_r)

    n_r, n_i = gather_rows()
    total = jnp.transpose(tcol[...])[:clusters]
    inverse = 1.0 / (total + pen)
    h_r = (n_r + g_r * total + goal[:clusters, :]) * inverse
    h_i = (n_i + g_i * total + goal[clusters:, :]) * inverse
    xs[:clusters, :] = g_r * h_r + g_i * h_i
    xs[clusters:rows2, :] = g_r * h_i - g_i * h_r
    xs[rows2:, :] = h_r * h_r + h_i * h_i
    g[:clusters, :] = h_r
    g[clusters:, :] = h_i

    def again(c):
        start = pl.multiple_of(c * span, span)
        at = pl.ds(start, span)
        f_r, f_i = times(er[at, :], ei[at, :], c, g)
        put(frh, frl, start, f_r)
        put(fih, fil, start, f_i)

    chunks(again)
    m_r, m_i = gather_rows()
    for k in range(clusters):
        w = power[k]
        for i in range(3):
            j = i * clusters + k
            t = w * xs[j : j + 1, :]
            t = sum(t[:, 128 * h : 128 * h + 128] for h in range(1, stations // 128)) + t[:, :128]
            sums[j : j + 1, :] = jnp.sum(jnp.transpose(t), axis=0, keepdims=True)
    t_0, t_1, t_2 = (sums[i * clusters : (i + 1) * clusters, :] for i in range(3))
    inverse = 1.0 / (t_2 + pen)
    new_r = (m_r + g_r * t_0 - g_i * t_1 + goal[:clusters, :]) * inverse
    new_i = (m_i + g_r * t_1 + g_i * t_0 + goal[clusters:, :]) * inverse
    new = jnp.concatenate([new_r, new_i], axis=0)
    gains[...] = new
    emit = pltpu.make_async_copy(gains, gains_out, outs.at[0])
    emit.start()

    spread = new + offset[...]
    each = stations // n_chan
    groups = rows2 // 8
    used = groups * each
    lanes = packed.shape[2]
    for j in range(n_chan):
        if used < lanes:
            packed[j] = jnp.zeros((8, lanes), f32)
        packed[j, :, :used] = jnp.concatenate(
            [spread[8 * i : 8 * i + 8, j * each : (j + 1) * each] for i in range(groups)], axis=1
        )
    first = []
    for j in range(1, n_chan):
        peer = lax.rem(me_c + n_chan - j, n_chan)
        first.append(send(packed.at[peer], zin.at[j], s1.at[j], r1.at[j], {"chan": peer}))
    for c in first:
        c.start()
    mixed = [packed[me_c] * taps[t][0:1, 0:1] for t in range(NTERM)]
    for j in range(1, n_chan):
        first[j - 1].wait_recv()
        got = zin[j]
        for t in range(NTERM):
            mixed[t] = mixed[t] + got * taps[t][j : j + 1, 0:1]
    wide = NTERM * each
    width = own.shape[1]
    if wide < width:
        own[...] = jnp.zeros_like(own)
    for i in range(groups):
        own[8 * i : 8 * i + 8, :wide] = jnp.concatenate(
            [mixed[t][:, i * each : (i + 1) * each] for t in range(NTERM)], axis=1
        )
    second = []
    for j in range(1, n_dir):
        peer = lax.rem(me_d + j, n_dir)
        second.append(send(own, zall.at[me_d], s2.at[j], r2.at[j], {"dir": peer}))
    for c in second:
        c.start()
    zall[me_d] = own[...]
    for c in second:
        c.wait()
    z_h, z_l = split(
        jnp.concatenate(
            [
                jnp.concatenate([zall[d][:clusters], zall[d][clusters:]], axis=1)
                for d in range(n_dir)
            ],
            axis=0,
        )
    )
    a = dot(hm[...], jnp.concatenate([z_h, z_l, z_h], axis=0))
    a_r, a_i = a[:, :width], a[:, width:]
    size = jnp.sqrt(a_r * a_r + a_i * a_i)
    limit = cut[0]
    scale = jnp.maximum(size - limit, 0.0) / jnp.maximum(size, limit)
    a_h, a_l = split(jnp.concatenate([a_r * scale, a_i * scale], axis=1)[:modes])
    m_h, m_l = split(harm[pl.ds(pl.multiple_of(me_d * clusters, clusters), clusters), :])
    twice = dot(jnp.concatenate([m_h, m_l], axis=0), a_h)
    done = twice[:clusters] + twice[clusters:] + dot(m_h, a_l)
    part[:clusters] = done[:, :width]
    part[clusters:] = done[:, width:]
    third = []
    for j in range(1, n_chan):
        peer = lax.rem(me_c + j, n_chan)
        third.append(send(part, blocks.at[me_c], s3.at[j], r3.at[j], {"chan": peer}))
    for c in third:
        c.start()
    keep = pltpu.make_async_copy(part, blocks.at[me_c], outs.at[1])
    keep.start()
    show = pltpu.make_async_copy(b_ref, band_out, outs.at[2])
    show.start()
    for c in gathers + first:
        c.wait_send()
    emit.wait()
    keep.wait()
    show.wait()
    for c in third:
        c.wait()


def emit_kernel(blocks, gains, dual, pen_ref, band, gains_out, dual_out, cons_out):
    n_chan, rows2, width = blocks.shape
    stations = gains.shape[1]
    each = stations // n_chan
    wide = NTERM * each
    level = legendre(band[0:1, 0:1])
    row = lax.broadcasted_iota(jnp.int32, (width, width), 0)
    col = lax.broadcasted_iota(jnp.int32, (width, width), 1)
    weave = jnp.zeros((width, width), f32)
    sample = jnp.zeros((width, width), f32)
    for t in range(NTERM):
        place = row - t * each
        inside = (place >= 0) & (place < each)
        weave = jnp.where(inside & (col == NTERM * place + t), 1.0, weave)
        sample = jnp.where(inside & (col == place), level[t], sample)
    s_h, s_l = split(sample)
    both = jnp.concatenate([weave.astype(bf16), s_h], axis=1)
    rest = jnp.concatenate([jnp.zeros((width, width), bf16), s_l], axis=1)
    b_h, b_l = split(jnp.concatenate([blocks[j] for j in range(n_chan)], axis=0))
    result = dot(
        jnp.concatenate([b_h, b_l, b_h], axis=1), jnp.concatenate([both, both, rest], axis=0)
    )
    fitted = []
    for j in range(n_chan):
        piece = result[j * rows2 : (j + 1) * rows2]
        cons_out[:, j * wide : (j + 1) * wide] = piece[:, :wide]
        fitted.append(piece[:, width : width + each])
    fitted = jnp.concatenate(fitted, axis=1)
    pen = column(pen_ref)
    pull = jnp.concatenate([pen, pen], axis=0)
    new = gains[...]
    fresh = halves(dual, rows2) + pull * (new - fitted)
    for j in range(2):
        gains_out[pl.ds(j, rows2, 2), :] = new[:, j * 128 : (j + 1) * 128]
        dual_out[pl.ds(j, rows2, 2), :] = fresh[:, j * 128 : (j + 1) * 128]


def solution(mesh):
    n_dir, n_chan = mesh.shape["dir"], mesh.shape["chan"]
    group = 2 if n_dir % 2 == 0 else 1

    def shards(
        visibilities, station_uv, source_lm, source_flux, band_offset, gains_init, duals_init,
        poly_init, penalty, harmonics, threshold,
    ):
        _, clusters, sources = source_lm.shape
        stations = station_uv.shape[1]
        modes = harmonics.shape[1]
        mode_rows = -(-modes // 128) * 128
        rows2 = 2 * clusters
        lanes = max(128, stations * NTERM // n_chan)
        flat = clusters * sources
        small = max(128, stations // n_chan * (rows2 // 8))
        vis = visibilities.reshape(stations, 2, stations // 128, 128)
        vis = vis.transpose(0, 2, 1, 3).reshape(stations * 4, 128)
        lines = rows2 * stations // 128
        dual = duals_init.reshape(lines, 128)
        pen = penalty.reshape(1, clusters)
        dma = pltpu.SemaphoreType.DMA
        vm = pltpu.VMEM
        wide16 = vm((flat, stations), bf16)
        long16 = vm((2 * flat, stations), bf16)
        per = n_dir // group
        gains, blocks, band = pl.pallas_call(
            functools.partial(step_kernel, n_dir, n_chan, group),
            out_shape=(
                jax.ShapeDtypeStruct((rows2, stations), f32),
                jax.ShapeDtypeStruct((n_chan, rows2, lanes), f32),
                jax.ShapeDtypeStruct((8, 128), f32),
            ),
            in_specs=[ANY] * 11,
            out_specs=(ANY,) * 3,
            scratch_shapes=[
                vm((stations * 4, 128), f32),
                vm(station_uv.shape, f32),
                vm(source_lm.shape, f32),
                vm(source_flux.shape, f32),
                pltpu.SMEM((1,), f32),
                vm((lines, 128), f32),
                vm((rows2, stations * NTERM), f32),
                vm(pen.shape, f32),
                vm(harmonics.shape, f32),
                pltpu.SMEM((1,), f32),
                vm((8, 128), f32),
                vm((n_chan, 8, 128), f32),
                vm((per, lines + sources, 128), f32),
                vm((flat, 128), f32),
                vm((rows2, stations), f32),
                vm((flat, stations), f32),
                vm((flat, stations), f32),
                wide16, wide16, wide16, wide16, wide16, wide16,
                long16, long16, long16, long16,
                wide16, wide16, wide16, wide16,
                vm((stations, stations), f32),
                vm((stations, stations), f32),
                vm((4, stations, 2 * stations), bf16),
                vm((clusters, stations, stations), f32),
                vm((3 * clusters, stations), f32),
                vm((3 * clusters, stations), f32),
                vm((stations, 128), f32),
                vm((rows2, stations), f32),
                vm((rows2, stations), f32),
                vm((mode_rows, 3 * harmonics.shape[0]), bf16),
                vm((n_chan, 8, small), f32),
                vm((n_chan, 8, small), f32),
                vm((rows2, lanes), f32),
                vm((n_dir, rows2, lanes), f32),
                vm((rows2, lanes), f32),
                vm((rows2, stations), f32),
                dma((11,)),
                dma((per,)), dma((per,)),
                dma((1,)), dma((1,)),
                dma((n_chan,)), dma((n_chan,)),
                dma((n_chan,)), dma((n_chan,)),
                dma((n_dir,)), dma((n_dir,)),
                dma((n_chan,)), dma((n_chan,)),
                dma((3,)),
            ],
            compiler_params=pltpu.CompilerParams(
                collective_id=0, has_side_effects=True, vmem_limit_bytes=62 * 2**20
            ),
            name="calibrate",
        )(
            vis, station_uv, source_lm, source_flux, band_offset, gains_init.reshape(lines, 128), dual,
            poly_init.reshape(rows2, stations * NTERM), pen, harmonics, threshold,
        )
        gains, duals, consensus = pl.pallas_call(
            emit_kernel,
            out_shape=(
                jax.ShapeDtypeStruct((lines, 128), f32),
                jax.ShapeDtypeStruct((lines, 128), f32),
                jax.ShapeDtypeStruct((rows2, stations * NTERM), f32),
            ),
            in_specs=[VM] * 5,
            out_specs=(VM,) * 3,
            name="emit",
        )(blocks, gains, dual, pen, band)
        shape = (2, clusters, 1, stations)
        return (
            gains.reshape(shape),
            duals.reshape(shape),
            consensus.reshape(2, clusters, stations * NTERM),
        )

    return jax.shard_map(
        shards,
        mesh=mesh,
        in_specs=(
            P("chan", None, None, None),
            P(),
            P(None, "dir", None),
            P("dir", None),
            P("chan"),
            P(None, "dir", "chan", None),
            P(None, "dir", "chan", None),
            P(None, "dir", None),
            P("dir"),
            P(),
            P(),
        ),
        out_specs=(
            P(None, "dir", "chan", None),
            P(None, "dir", "chan", None),
            P(None, "dir", None),
        ),
        check_vma=False,
    )
```

```python
import functools

import jax
import jax.numpy as jnp
import numpy as np
from jax import lax
from jax.experimental import pallas as pl
from jax.experimental.pallas import tpu as pltpu
from jax.sharding import PartitionSpec as P

NTERM = 4
MESH = pl.DeviceIdType.MESH
VM = pl.BlockSpec(memory_space=pltpu.VMEM)
ANY = pl.BlockSpec(memory_space=pltpu.HBM)
f32, bf16 = jnp.float32, jnp.bfloat16


def fit_half_circle():
    nodes = np.cos(np.pi * (np.arange(400) + 0.5) / 800.0) * 0.5
    square = nodes * nodes
    fit = np.polynomial.chebyshev.Chebyshev.fit
    root = np.sqrt(2.0)
    sine = fit(square, root * np.sin(np.pi * nodes) / nodes, 3, domain=[0, 0.25], w=nodes)
    cosine = fit(square, root * np.cos(np.pi * nodes), 4, domain=[0, 0.25])
    kind = np.polynomial.Polynomial
    return [[float(c) for c in p.convert(kind=kind).coef] for p in (sine, cosine)]


SINE, COSINE = fit_half_circle()


def horner(coefs, x):
    total = coefs[-1] * x + coefs[-2]
    for c in coefs[-3::-1]:
        total = total * x + c
    return total


def legendre(x):
    return [
        jnp.ones_like(x),
        x,
        0.5 * (3.0 * x * x - 1.0),
        0.5 * (5.0 * x * x * x - 3.0 * x),
    ]


def split(x):
    high = x.astype(bf16)
    low = (x - high.astype(f32)).astype(bf16)
    return high, low


def dot(a, b):
    return jnp.dot(a, b, preferred_element_type=f32)


def tdot(a, b):
    return lax.dot_general(a, b, (((0,), (0,)), ((), ())), preferred_element_type=f32)


def column(pen):
    count = pen.shape[1]
    row = lax.broadcasted_iota(jnp.int32, (count, count), 0)
    col = lax.broadcasted_iota(jnp.int32, (count, count), 1)
    return jnp.sum(jnp.where(row == col, pen[...], 0.0), axis=1, keepdims=True)


def halves(ref, rows):
    return jnp.concatenate([ref[pl.ds(j, rows, 2), :] for j in range(2)], axis=1)


def fit_taps(values):
    gram = [
        [jnp.sum(values[t] * values[s], axis=0, keepdims=True) for s in range(t + 1)]
        for t in range(NTERM)
    ]
    factor = [[None] * NTERM for _ in range(NTERM)]
    for t in range(NTERM):
        for s in range(t + 1):
            rest = gram[t][s]
            for r in range(s):
                rest = rest - factor[t][r] * factor[s][r]
            factor[t][s] = jnp.sqrt(rest) if s == t else rest / factor[s][s]
    half = []
    for t in range(NTERM):
        rest = values[t]
        for s in range(t):
            rest = rest - factor[t][s] * half[s]
        half.append(rest / factor[t][t])
    taps = [None] * NTERM
    for t in reversed(range(NTERM)):
        rest = half[t]
        for s in range(t + 1, NTERM):
            rest = rest - factor[s][t] * taps[s]
        taps[t] = rest / factor[t][t]
    return taps


def step_kernel(
    n_dir, n_chan, group,
    vis_hbm, uv_hbm, lm_hbm, flux_hbm, band_hbm, g_hbm, dual_hbm, poly_hbm, pen_hbm, harm_hbm,
    cut_hbm,
    gains_out, blocks, band_out,
    vis, uv, lm, flux, band, dual, poly, pen_ref, harm, cut,
    b_ref, b_all, pack, src, g, er, ei,
    erh, erl, eih, eil, nih, nil,
    frh, frl, fih, fil, drh, drl, srh, srl,
    partial, partner,
    rs, power, xs, sums, tcol, goal, offset, hm,
    packed, zin, part, gains,
    ins, gs, gr, ms, mr, bs, br, s1, r1, s3, r3, outs,
):
    rows2, stations = g.shape
    clusters = rows2 // 2
    sources = er.shape[0] // clusters
    flat = clusters * sources
    me_d, me_c = lax.axis_index("dir"), lax.axis_index("chan")
    barrier = pltpu.get_barrier_semaphore()
    members = n_dir * n_chan

    def everyone(body):
        if members <= 64:
            for i in range(1, members):
                body(i // n_chan, i % n_chan)
        else:

            def step(i, carry):
                body(i // n_chan, i % n_chan)
                return carry

            lax.fori_loop(1, members, step, 0)

    for j in range(1, n_dir):
        pl.semaphore_signal(
            barrier, inc=1, device_id={"dir": lax.rem(me_d + j, n_dir)}, device_id_type=MESH
        )
    for j in range(1, n_chan):
        pl.semaphore_signal(
            barrier, inc=1, device_id={"chan": lax.rem(me_c + j, n_chan)}, device_id_type=MESH
        )
    loads = [
        pltpu.make_async_copy(a, b, ins.at[i])
        for i, (a, b) in enumerate(
            [
                (band_hbm, band),
                (lm_hbm, lm),
                (flux_hbm, flux),
                (g_hbm, pack.at[0, : 4 * clusters]),
                (uv_hbm, uv),
                (cut_hbm, cut),
                (dual_hbm, dual),
                (poly_hbm, poly),
                (pen_hbm, pen_ref),
                (harm_hbm, harm),
                (vis_hbm, vis),
            ]
        )
    ]
    for c in loads:
        c.start()

    def send(s, d, a, b, peer):
        return pltpu.make_async_remote_copy(
            src_ref=s, dst_ref=d, send_sem=a, recv_sem=b, device_id=peer, device_id_type=MESH
        )

    for c in loads[:5]:
        c.wait()
    table = jnp.concatenate([lm[0], lm[1], jnp.sqrt(flux[...])], axis=0)
    fill = (-3 * clusters) % 128
    table = jnp.concatenate([table, jnp.zeros((fill, sources), f32)], axis=0)
    pack[0, 4 * clusters : 4 * clusters + sources, :] = jnp.transpose(table)
    here = jnp.full((1, 1), band[0], f32)
    b_ref[...] = jnp.full(b_ref.shape, band[0], f32)
    b_all[0] = b_ref[...]
    stretch = 1.0 + 0.25 * here
    u = uv[0:1, :] * stretch
    v = uv[1:2, :] * stretch

    def open_pack(slot):
        g_all = halves(pack.at[slot, : 4 * clusters], rows2)
        g[...] = g_all
        t = pack[slot, 4 * clusters : 4 * clusters + sources, :]
        for k in range(clusters):
            src[k * sources : (k + 1) * sources, :] = pltpu.roll(t, (128 - k) % 128, 1)
        return g_all

    chunk = 4
    span = chunk * sources

    def circle(start):
        cols = src[pl.ds(start, span), :]
        turns = cols[:, 0:1] * u + cols[:, clusters : clusters + 1] * v
        r = turns - jnp.round(turns)
        square = r * r
        s = r * horner(SINE, square)
        c = horner(COSINE, square)
        w = cols[:, 2 * clusters : 2 * clusters + 1]
        ws = w * s
        return w - ws * s, ws * c

    def times(e_r, e_i, c, ref):
        f_r, f_i = [], []
        for i in range(chunk):
            a = ref[pl.ds(c * chunk + i, 1), :]
            b = ref[pl.ds(clusters + c * chunk + i, 1), :]
            p_r = e_r[i * sources : (i + 1) * sources]
            p_i = e_i[i * sources : (i + 1) * sources]
            f_r.append(p_r * a - p_i * b)
            f_i.append(p_r * b + p_i * a)
        return jnp.concatenate(f_r, axis=0), jnp.concatenate(f_i, axis=0)

    def put(h_ref, l_ref, start, x):
        h, l = split(x)
        h_ref[pl.ds(start, span), :] = h
        l_ref[pl.ds(start, span), :] = l
        return h, l

    def field_chunk(c, keep):
        start = pl.multiple_of(c * span, span)
        e_r, e_i = circle(start)
        if keep:
            er[pl.ds(start, span), :] = e_r
            ei[pl.ds(start, span), :] = e_i
            put(erh, erl, start, e_r)
            h, l = put(eih, eil, start, e_i)
            nih[pl.ds(start, span), :] = -h
            nil[pl.ds(start, span), :] = -l
        f_r, f_i = times(e_r, e_i, c, g)
        off = 0 if keep else flat
        put(frh, frl, start + off, f_r)
        put(fih, fil, start + off, f_i)
        put(drh, drl, start, f_r - f_i)
        put(srh, srl, start, f_i + f_r)

    lane = lax.broadcasted_iota(jnp.int32, (stations, 128), 1)

    def power_chunk(c):
        acc = tcol[...]
        for i in range(chunk):
            k = c * chunk + i
            at = pl.ds(pl.multiple_of(k * sources, sources), sources)
            r_h, r_l, i_h, i_l = erh[at, :], erl[at, :], eih[at, :], eil[at, :]
            n_h, n_l = nih[at, :], nil[at, :]
            left = jnp.concatenate([r_h, i_h, r_h, i_h, r_l, i_l], axis=0)
            real = jnp.concatenate([r_h, i_h, r_l, i_l, r_h, i_h], axis=0)
            imag = jnp.concatenate([n_h, r_h, n_l, r_l, n_h, r_h], axis=0)
            both = tdot(left, jnp.concatenate([real, imag], axis=1))
            c_r, c_i = both[:, :stations], both[:, stations:]
            w = c_r * c_r + c_i * c_i
            power[k] = w
            t = jnp.sum(w * xs[pl.ds(k, 1), :], axis=1, keepdims=True)
            acc = jnp.where(lane == k, t, acc)
        tcol[...] = acc

    def chunks(body, low=0, high=clusters // chunk):
        def step(c, carry):
            body(c)
            return carry

        lax.fori_loop(low, high, step, 0)

    def model(off):
        def rows(a, b):
            return jnp.concatenate([a[off : off + flat, :], b[off : off + flat, :]], axis=0)

        d_h = jnp.concatenate([drh[...], srh[...]], axis=0)
        d_l = jnp.concatenate([drl[...], srl[...]], axis=0)
        first = tdot(rows(frh, fih), jnp.concatenate([d_h, d_l], axis=1))
        second = tdot(rows(frl, fil), d_h)
        return first[:, :stations] + first[:, stations:] + second

    g_own = open_pack(0)
    g_r, g_i = g_own[:clusters], g_own[clusters:]
    xs[:clusters, :] = g_r * g_r + g_i * g_i
    tcol[...] = jnp.zeros((stations, 128), f32)
    chunks(lambda c: field_chunk(c, True), 0, 2)

    pl.semaphore_wait(barrier, n_dir + n_chan - 2)
    per = n_dir // group
    gathers = []
    for j in range(1, per):
        peer = {"dir": lax.rem(me_d + n_dir - group * j, n_dir)}
        gathers.append(send(pack.at[0], pack.at[j], gs.at[j], gr.at[j], peer))
    bands = []
    for j in range(1, n_chan):
        peer = {"chan": lax.rem(me_c + n_chan - j, n_chan)}
        bands.append(send(b_ref, b_all.at[j], bs.at[j], br.at[j], peer))
    for c in gathers + bands:
        c.start()

    chunks(lambda c: field_chunk(c, True), 2)
    partial[...] = model(0)

    def first_other(c):
        field_chunk(c, False)
        power_chunk(c)

    if per > 1:
        gathers[0].wait_recv()
        open_pack(1)
        chunks(first_other)
        partial[...] += model(flat)
    else:
        chunks(power_chunk)

    def others(j, carry):
        for i in range(2, per):

            @pl.when(j == i)
            def _():
                gathers[i - 1].wait_recv()

        open_pack(j)
        chunks(lambda c: field_chunk(c, False))
        partial[...] += model(flat)
        return carry

    if per > 2:
        lax.fori_loop(2, per, others, 0)
    if group == 2:
        mate = {"dir": me_d + 1 - 2 * lax.rem(me_d, 2)}
        swap = send(partial, partner, ms.at[0], mr.at[0], mate)
        swap.start()

    for c in loads[5:10]:
        c.wait()
    level = legendre(here)
    pen = column(pen_ref)
    pull = jnp.concatenate([pen, pen], axis=0)
    tile = 32 * NTERM
    tiles = stations // 32
    row = lax.broadcasted_iota(jnp.int32, (tile, tile), 0)
    col = lax.broadcasted_iota(jnp.int32, (tile, tile), 1)
    pick = jnp.zeros((tile, tile), f32)
    for t in range(NTERM):
        pick = jnp.where(row - NTERM * col == t, level[t], pick)
    p_h, p_l = split(pick)
    q_h, q_l = split(
        jnp.concatenate([poly[:, j * tile : (j + 1) * tile] for j in range(tiles)], axis=0)
    )
    value = dot(
        jnp.concatenate([q_h, q_l, q_h], axis=1), jnp.concatenate([p_h, p_h, p_l], axis=0)
    )
    value = jnp.concatenate(
        [value[j * rows2 : (j + 1) * rows2, :32] for j in range(tiles)], axis=1
    )
    offset[...] = halves(dual, rows2) / pull
    goal[...] = (value - offset[...]) * pull
    modes = harm.shape[1]

    def mode_block(a):
        start = lax.rem(me_d + a, n_dir) * clusters
        return harm[pl.ds(pl.multiple_of(start, clusters), clusters), :]

    mode_rows = hm.shape[0]
    turned = jnp.concatenate([mode_block(a) for a in range(n_dir)], axis=0)
    turned = jnp.concatenate(
        [turned, jnp.zeros((turned.shape[0], mode_rows - modes), f32)], axis=1
    )
    h_h, h_l = split(jnp.transpose(turned))
    hm[...] = jnp.concatenate([h_h, h_h, h_l], axis=1)
    for c in bands:
        c.wait()
    taps = fit_taps(legendre(b_all[:, 0, :]))

    loads[10].wait()
    if group == 2:
        swap.wait()
        both = partial[...] + partner[...]
    else:
        both = partial[...]
    turned = jnp.transpose(both)

    def seen(i):
        return jnp.concatenate(
            [vis[pl.ds(2 * j + i, stations, 4), :] for j in range(2)], axis=1
        )

    r_h, r_l = split(seen(0) - 0.5 * (both + turned))
    i_h, i_l = split(seen(1) - 0.5 * (both - turned))
    rs[0, :, :stations] = r_h
    rs[0, :, stations:] = -i_h
    rs[1, :, :stations] = i_h
    rs[1, :, stations:] = r_h
    rs[2, :, :stations] = r_l
    rs[2, :, stations:] = -i_l
    rs[3, :, :stations] = i_l
    rs[3, :, stations:] = r_l

    def gather_rows():
        a, b = frh[:flat, :], fih[:flat, :]
        y = dot(
            jnp.concatenate([a, b, a, b, frl[:flat, :], fil[:flat, :]], axis=1),
            jnp.concatenate([rs[0], rs[1], rs[2], rs[3], rs[0], rs[1]], axis=0),
        )
        y_r, y_i = y[:, :stations], y[:, stations:]
        e_r, e_i = er[...], ei[...]

        def over(x):
            return jnp.sum(x.reshape(clusters, sources, stations), axis=1)

        return over(e_r * y_r + e_i * y_i), over(e_r * y_i - e_i * y_r)

    n_r, n_i = gather_rows()
    total = jnp.transpose(tcol[...])[:clusters]
    inverse = 1.0 / (total + pen)
    h_r = (n_r + g_r * total + goal[:clusters, :]) * inverse
    h_i = (n_i + g_i * total + goal[clusters:, :]) * inverse
    xs[:clusters, :] = g_r * h_r + g_i * h_i
    xs[clusters:rows2, :] = g_r * h_i - g_i * h_r
    xs[rows2:, :] = h_r * h_r + h_i * h_i
    g[:clusters, :] = h_r
    g[clusters:, :] = h_i

    def again(c):
        start = pl.multiple_of(c * span, span)
        at = pl.ds(start, span)
        f_r, f_i = times(er[at, :], ei[at, :], c, g)
        put(frh, frl, start, f_r)
        put(fih, fil, start, f_i)

    chunks(again)
    m_r, m_i = gather_rows()
    for k in range(clusters):
        w = power[k]
        for i in range(3):
            j = i * clusters + k
            t = w * xs[j : j + 1, :]
            t = sum(t[:, 128 * h : 128 * h + 128] for h in range(1, stations // 128)) + t[:, :128]
            sums[j : j + 1, :] = jnp.sum(jnp.transpose(t), axis=0, keepdims=True)
    t_0, t_1, t_2 = (sums[i * clusters : (i + 1) * clusters, :] for i in range(3))
    inverse = 1.0 / (t_2 + pen)
    new_r = (m_r + g_r * t_0 - g_i * t_1 + goal[:clusters, :]) * inverse
    new_i = (m_i + g_r * t_1 + g_i * t_0 + goal[clusters:, :]) * inverse
    new = jnp.concatenate([new_r, new_i], axis=0)
    gains[...] = new
    emit = pltpu.make_async_copy(gains, gains_out, outs.at[0])
    emit.start()

    spread = new + offset[...]
    each = stations // n_chan
    groups = rows2 // 8
    used = groups * each
    lanes = packed.shape[2]
    for j in range(n_chan):
        if used < lanes:
            packed[j] = jnp.zeros((8, lanes), f32)
        packed[j, :, :used] = jnp.concatenate(
            [spread[8 * i : 8 * i + 8, j * each : (j + 1) * each] for i in range(groups)], axis=1
        )
    def moment(a, j):
        to_d, to_c = lax.rem(me_d + n_dir - a, n_dir), lax.rem(me_c + n_chan - j, n_chan)
        return send(
            packed.at[to_c], zin.at[a, j], s1.at[a, j], r1.at[a, j], {"dir": to_d, "chan": to_c}
        )

    everyone(lambda a, j: moment(a, j).start())
    wide = NTERM * each
    width = part.shape[1]
    rows = []
    for a in range(n_dir):
        mixed = [None] * NTERM
        for j in range(n_chan):
            if a == j == 0:
                got = packed[me_c]
            else:
                moment(a, j).wait_recv()
                got = zin[a, j]
            for t in range(NTERM):
                term = got * taps[t][j : j + 1, 0:1]
                mixed[t] = term if j == 0 else mixed[t] + term

        def terms(i):
            row = [mixed[t][:, i * each : (i + 1) * each] for t in range(NTERM)]
            if wide < width:
                row.append(jnp.zeros((8, width - wide), f32))
            return jnp.concatenate(row, axis=1)

        tall = groups // 2
        rows.append(
            jnp.concatenate(
                [
                    jnp.concatenate([terms(r * tall + i) for i in range(tall)], axis=0)
                    for r in range(2)
                ],
                axis=1,
            )
        )
    z_h, z_l = split(jnp.concatenate(rows, axis=0))
    a = dot(hm[...], jnp.concatenate([z_h, z_l, z_h], axis=0))
    a_r, a_i = a[:, :width], a[:, width:]
    size = jnp.sqrt(a_r * a_r + a_i * a_i)
    limit = cut[0]
    scale = jnp.maximum(size - limit, 0.0) / jnp.maximum(size, limit)
    a_h, a_l = split(jnp.concatenate([a_r * scale, a_i * scale], axis=1)[:modes])
    m_h, m_l = split(mode_block(0))
    twice = dot(jnp.concatenate([m_h, m_l], axis=0), a_h)
    done = twice[:clusters] + twice[clusters:] + dot(m_h, a_l)
    part[:clusters] = done[:, :width]
    part[clusters:] = done[:, width:]
    third = []
    for j in range(1, n_chan):
        peer = lax.rem(me_c + j, n_chan)
        third.append(send(part, blocks.at[me_c], s3.at[j], r3.at[j], {"chan": peer}))
    for c in third:
        c.start()
    keep = pltpu.make_async_copy(part, blocks.at[me_c], outs.at[1])
    keep.start()
    show = pltpu.make_async_copy(b_ref, band_out, outs.at[2])
    show.start()
    for c in gathers:
        c.wait_send()
    everyone(lambda a, j: moment(a, j).wait_send())
    emit.wait()
    keep.wait()
    show.wait()
    for c in third:
        c.wait()


def emit_kernel(blocks, gains, dual, pen_ref, band, gains_out, dual_out, cons_out):
    n_chan, rows2, width = blocks.shape
    stations = gains.shape[1]
    each = stations // n_chan
    wide = NTERM * each
    level = legendre(band[0:1, 0:1])
    row = lax.broadcasted_iota(jnp.int32, (width, width), 0)
    col = lax.broadcasted_iota(jnp.int32, (width, width), 1)
    weave = jnp.zeros((width, width), f32)
    sample = jnp.zeros((width, width), f32)
    for t in range(NTERM):
        place = row - t * each
        inside = (place >= 0) & (place < each)
        weave = jnp.where(inside & (col == NTERM * place + t), 1.0, weave)
        sample = jnp.where(inside & (col == place), level[t], sample)
    s_h, s_l = split(sample)
    both = jnp.concatenate([weave.astype(bf16), s_h], axis=1)
    rest = jnp.concatenate([jnp.zeros((width, width), bf16), s_l], axis=1)
    b_h, b_l = split(jnp.concatenate([blocks[j] for j in range(n_chan)], axis=0))
    result = dot(
        jnp.concatenate([b_h, b_l, b_h], axis=1), jnp.concatenate([both, both, rest], axis=0)
    )
    fitted = []
    for j in range(n_chan):
        piece = result[j * rows2 : (j + 1) * rows2]
        cons_out[:, j * wide : (j + 1) * wide] = piece[:, :wide]
        fitted.append(piece[:, width : width + each])
    fitted = jnp.concatenate(fitted, axis=1)
    pen = column(pen_ref)
    pull = jnp.concatenate([pen, pen], axis=0)
    new = gains[...]
    fresh = halves(dual, rows2) + pull * (new - fitted)
    for j in range(2):
        gains_out[pl.ds(j, rows2, 2), :] = new[:, j * 128 : (j + 1) * 128]
        dual_out[pl.ds(j, rows2, 2), :] = fresh[:, j * 128 : (j + 1) * 128]


def solution(mesh):
    n_dir, n_chan = mesh.shape["dir"], mesh.shape["chan"]
    group = 2 if n_dir % 2 == 0 else 1

    def shards(
        visibilities, station_uv, source_lm, source_flux, band_offset, gains_init, duals_init,
        poly_init, penalty, harmonics, threshold,
    ):
        _, clusters, sources = source_lm.shape
        stations = station_uv.shape[1]
        modes = harmonics.shape[1]
        mode_rows = -(-modes // 128) * 128
        rows2 = 2 * clusters
        lanes = max(128, stations * NTERM // n_chan)
        flat = clusters * sources
        small = max(128, stations // n_chan * (rows2 // 8))
        vis = visibilities.reshape(stations, 2, stations // 128, 128)
        vis = vis.transpose(0, 2, 1, 3).reshape(stations * 4, 128)
        lines = rows2 * stations // 128
        dual = duals_init.reshape(lines, 128)
        pen = penalty.reshape(1, clusters)
        dma = pltpu.SemaphoreType.DMA
        vm = pltpu.VMEM
        wide16 = vm((flat, stations), bf16)
        long16 = vm((2 * flat, stations), bf16)
        per = n_dir // group
        gains, blocks, band = pl.pallas_call(
            functools.partial(step_kernel, n_dir, n_chan, group),
            out_shape=(
                jax.ShapeDtypeStruct((rows2, stations), f32),
                jax.ShapeDtypeStruct((n_chan, rows2, lanes), f32),
                jax.ShapeDtypeStruct((8, 128), f32),
            ),
            in_specs=[ANY] * 11,
            out_specs=(ANY,) * 3,
            scratch_shapes=[
                vm((stations * 4, 128), f32),
                vm(station_uv.shape, f32),
                vm(source_lm.shape, f32),
                vm(source_flux.shape, f32),
                pltpu.SMEM((1,), f32),
                vm((lines, 128), f32),
                vm((rows2, stations * NTERM), f32),
                vm(pen.shape, f32),
                vm(harmonics.shape, f32),
                pltpu.SMEM((1,), f32),
                vm((8, 128), f32),
                vm((n_chan, 8, 128), f32),
                vm((per, lines + sources, 128), f32),
                vm((flat, 128), f32),
                vm((rows2, stations), f32),
                vm((flat, stations), f32),
                vm((flat, stations), f32),
                wide16, wide16, wide16, wide16, wide16, wide16,
                long16, long16, long16, long16,
                wide16, wide16, wide16, wide16,
                vm((stations, stations), f32),
                vm((stations, stations), f32),
                vm((4, stations, 2 * stations), bf16),
                vm((clusters, stations, stations), f32),
                vm((3 * clusters, stations), f32),
                vm((3 * clusters, stations), f32),
                vm((stations, 128), f32),
                vm((rows2, stations), f32),
                vm((rows2, stations), f32),
                vm((mode_rows, 3 * harmonics.shape[0]), bf16),
                vm((n_chan, 8, small), f32),
                vm((n_dir, n_chan, 8, small), f32),
                vm((rows2, lanes), f32),
                vm((rows2, stations), f32),
                dma((11,)),
                dma((per,)), dma((per,)),
                dma((1,)), dma((1,)),
                dma((n_chan,)), dma((n_chan,)),
                dma((n_dir, n_chan)), dma((n_dir, n_chan)),
                dma((n_chan,)), dma((n_chan,)),
                dma((3,)),
            ],
            compiler_params=pltpu.CompilerParams(
                collective_id=0, has_side_effects=True, vmem_limit_bytes=62 * 2**20
            ),
            name="calibrate",
        )(
            vis, station_uv, source_lm, source_flux, band_offset, gains_init.reshape(lines, 128), dual,
            poly_init.reshape(rows2, stations * NTERM), pen, harmonics, threshold,
        )
        gains, duals, consensus = pl.pallas_call(
            emit_kernel,
            out_shape=(
                jax.ShapeDtypeStruct((lines, 128), f32),
                jax.ShapeDtypeStruct((lines, 128), f32),
                jax.ShapeDtypeStruct((rows2, stations * NTERM), f32),
            ),
            in_specs=[VM] * 5,
            out_specs=(VM,) * 3,
            name="emit",
        )(blocks, gains, dual, pen, band)
        shape = (2, clusters, 1, stations)
        return (
            gains.reshape(shape),
            duals.reshape(shape),
            consensus.reshape(2, clusters, stations * NTERM),
        )

    return jax.shard_map(
        shards,
        mesh=mesh,
        in_specs=(
            P("chan", None, None, None),
            P(),
            P(None, "dir", None),
            P("dir", None),
            P("chan"),
            P(None, "dir", "chan", None),
            P(None, "dir", "chan", None),
            P(None, "dir", None),
            P("dir"),
            P(),
            P(),
        ),
        out_specs=(
            P(None, "dir", "chan", None),
            P(None, "dir", "chan", None),
            P(None, "dir", None),
        ),
        check_vma=False,
    )
```

```python
import functools

import jax
import jax.numpy as jnp
import numpy as np
from jax import lax
from jax.experimental import pallas as pl
from jax.experimental.pallas import tpu as pltpu
from jax.sharding import PartitionSpec as P

NTERM = 4
MESH = pl.DeviceIdType.MESH
VM = pl.BlockSpec(memory_space=pltpu.VMEM)
ANY = pl.BlockSpec(memory_space=pltpu.HBM)
f32, bf16 = jnp.float32, jnp.bfloat16


def fit_half_circle():
    nodes = np.cos(np.pi * (np.arange(400) + 0.5) / 800.0) * 0.5
    square = nodes * nodes
    fit = np.polynomial.chebyshev.Chebyshev.fit
    root = np.sqrt(2.0)
    sine = fit(square, root * np.sin(np.pi * nodes) / nodes, 3, domain=[0, 0.25], w=nodes)
    cosine = fit(square, root * np.cos(np.pi * nodes), 4, domain=[0, 0.25])
    kind = np.polynomial.Polynomial
    return [[float(c) for c in p.convert(kind=kind).coef] for p in (sine, cosine)]


SINE, COSINE = fit_half_circle()


def horner(coefs, x):
    total = coefs[-1] * x + coefs[-2]
    for c in coefs[-3::-1]:
        total = total * x + c
    return total


def legendre(x):
    return [
        jnp.ones_like(x),
        x,
        0.5 * (3.0 * x * x - 1.0),
        0.5 * (5.0 * x * x * x - 3.0 * x),
    ]


def split(x):
    high = x.astype(bf16)
    low = (x - high.astype(f32)).astype(bf16)
    return high, low


def dot(a, b):
    return jnp.dot(a, b, preferred_element_type=f32)


def tdot(a, b):
    return lax.dot_general(a, b, (((0,), (0,)), ((), ())), preferred_element_type=f32)


def column(pen):
    count = pen.shape[1]
    row = lax.broadcasted_iota(jnp.int32, (count, count), 0)
    col = lax.broadcasted_iota(jnp.int32, (count, count), 1)
    return jnp.sum(jnp.where(row == col, pen[...], 0.0), axis=1, keepdims=True)


def halves(ref, rows):
    return jnp.concatenate([ref[pl.ds(j, rows, 2), :] for j in range(2)], axis=1)


def fit_taps(values):
    gram = [
        [jnp.sum(values[t] * values[s], axis=0, keepdims=True) for s in range(t + 1)]
        for t in range(NTERM)
    ]
    factor = [[None] * NTERM for _ in range(NTERM)]
    for t in range(NTERM):
        for s in range(t + 1):
            rest = gram[t][s]
            for r in range(s):
                rest = rest - factor[t][r] * factor[s][r]
            factor[t][s] = jnp.sqrt(rest) if s == t else rest / factor[s][s]
    half = []
    for t in range(NTERM):
        rest = values[t]
        for s in range(t):
            rest = rest - factor[t][s] * half[s]
        half.append(rest / factor[t][t])
    taps = [None] * NTERM
    for t in reversed(range(NTERM)):
        rest = half[t]
        for s in range(t + 1, NTERM):
            rest = rest - factor[s][t] * taps[s]
        taps[t] = rest / factor[t][t]
    return taps


def step_kernel(
    n_dir, n_chan, group,
    vis_hbm, uv_hbm, lm_hbm, flux_hbm, band_hbm, g_hbm, dual_hbm, poly_hbm, pen_hbm, harm_hbm,
    cut_hbm,
    gains_out, blocks, band_out,
    vis, uv, lm, flux, band, dual, poly, pen_ref, harm, cut,
    b_ref, b_all, pack, src, g, er, ei,
    erh, erl, eih, eil, nih, nil,
    frh, frl, fih, fil, drh, drl, srh, srl,
    partial, partner,
    rs, power, ones, xs, sums, tcol, goal, offset, hm,
    packed, zin, part, gains,
    ins, gs, gr, ms, mr, bs, br, s1, r1, s3, r3, outs,
):
    rows2, stations = g.shape
    clusters = rows2 // 2
    sources = er.shape[0] // clusters
    flat = clusters * sources
    me_d, me_c = lax.axis_index("dir"), lax.axis_index("chan")
    barrier = pltpu.get_barrier_semaphore()
    members = n_dir * n_chan

    def everyone(body):
        if members <= 64:
            for i in range(1, members):
                body(i // n_chan, i % n_chan)
        else:

            def step(i, carry):
                body(i // n_chan, i % n_chan)
                return carry

            lax.fori_loop(1, members, step, 0)

    for j in range(1, n_dir):
        pl.semaphore_signal(
            barrier, inc=1, device_id={"dir": lax.rem(me_d + j, n_dir)}, device_id_type=MESH
        )
    for j in range(1, n_chan):
        pl.semaphore_signal(
            barrier, inc=1, device_id={"chan": lax.rem(me_c + j, n_chan)}, device_id_type=MESH
        )
    loads = [
        pltpu.make_async_copy(a, b, ins.at[i])
        for i, (a, b) in enumerate(
            [
                (band_hbm, band),
                (lm_hbm, lm),
                (flux_hbm, flux),
                (g_hbm, pack.at[0, : 4 * clusters]),
                (uv_hbm, uv),
                (cut_hbm, cut),
                (dual_hbm, dual),
                (poly_hbm, poly),
                (pen_hbm, pen_ref),
                (harm_hbm, harm),
                (vis_hbm, vis),
            ]
        )
    ]
    for c in loads:
        c.start()

    def send(s, d, a, b, peer):
        return pltpu.make_async_remote_copy(
            src_ref=s, dst_ref=d, send_sem=a, recv_sem=b, device_id=peer, device_id_type=MESH
        )

    for c in loads[:5]:
        c.wait()
    table = jnp.concatenate([lm[0], lm[1], jnp.sqrt(flux[...])], axis=0)
    fill = (-3 * clusters) % 128
    table = jnp.concatenate([table, jnp.zeros((fill, sources), f32)], axis=0)
    pack[0, 4 * clusters : 4 * clusters + sources, :] = jnp.transpose(table)
    here = jnp.full((1, 1), band[0], f32)
    b_ref[...] = jnp.full(b_ref.shape, band[0], f32)
    b_all[0] = b_ref[...]
    stretch = 1.0 + 0.25 * here
    u = uv[0:1, :] * stretch
    v = uv[1:2, :] * stretch

    def open_pack(slot):
        g_all = halves(pack.at[slot, : 4 * clusters], rows2)
        g[...] = g_all
        t = pack[slot, 4 * clusters : 4 * clusters + sources, :]
        for k in range(clusters):
            src[k * sources : (k + 1) * sources, :] = pltpu.roll(t, (128 - k) % 128, 1)
        return g_all

    chunk = 4
    span = chunk * sources

    def circle(start):
        cols = src[pl.ds(start, span), :]
        turns = cols[:, 0:1] * u + cols[:, clusters : clusters + 1] * v
        r = turns - jnp.round(turns)
        square = r * r
        s = r * horner(SINE, square)
        c = horner(COSINE, square)
        w = cols[:, 2 * clusters : 2 * clusters + 1]
        ws = w * s
        return w - ws * s, ws * c

    def times(e_r, e_i, c, ref):
        f_r, f_i = [], []
        for i in range(chunk):
            a = ref[pl.ds(c * chunk + i, 1), :]
            b = ref[pl.ds(clusters + c * chunk + i, 1), :]
            p_r = e_r[i * sources : (i + 1) * sources]
            p_i = e_i[i * sources : (i + 1) * sources]
            f_r.append(p_r * a - p_i * b)
            f_i.append(p_r * b + p_i * a)
        return jnp.concatenate(f_r, axis=0), jnp.concatenate(f_i, axis=0)

    def put(h_ref, l_ref, start, x):
        h, l = split(x)
        h_ref[pl.ds(start, span), :] = h
        l_ref[pl.ds(start, span), :] = l
        return h, l

    def field_chunk(c, keep):
        start = c * span if isinstance(c, int) else pl.multiple_of(c * span, span)
        e_r, e_i = circle(start)
        if keep:
            er[pl.ds(start, span), :] = e_r
            ei[pl.ds(start, span), :] = e_i
            put(erh, erl, start, e_r)
            h, l = put(eih, eil, start, e_i)
            nih[pl.ds(start, span), :] = -h
            nil[pl.ds(start, span), :] = -l
        f_r, f_i = times(e_r, e_i, c, g)
        off = 0 if keep else flat
        put(frh, frl, start + off, f_r)
        put(fih, fil, start + off, f_i)
        put(drh, drl, start, f_r - f_i)
        put(srh, srl, start, f_i + f_r)

    lane = lax.broadcasted_iota(jnp.int32, (stations, 128), 1)

    def power_chunk(c):
        acc = tcol[...]
        for i in range(chunk):
            k = c * chunk + i
            at = k * sources
            at = pl.ds(at if isinstance(k, int) else pl.multiple_of(at, sources), sources)
            r_h, r_l, i_h, i_l = erh[at, :], erl[at, :], eih[at, :], eil[at, :]
            n_h, n_l = nih[at, :], nil[at, :]
            left = jnp.concatenate([r_h, i_h, r_h, i_h, r_l, i_l], axis=0)
            real = jnp.concatenate([r_h, i_h, r_l, i_l, r_h, i_h], axis=0)
            imag = jnp.concatenate([n_h, r_h, n_l, r_l, n_h, r_h], axis=0)
            both = tdot(left, jnp.concatenate([real, imag], axis=1))
            c_r, c_i = both[:, :stations], both[:, stations:]
            w = c_r * c_r + c_i * c_i
            power[k] = w
            t = jnp.sum(w * xs[pl.ds(k, 1), :], axis=1, keepdims=True)
            acc = jnp.where(lane == k, t, acc)
        tcol[...] = acc

    def chunks(body, low=0, high=clusters // chunk):
        def step(c, carry):
            body(c)
            return carry

        lax.fori_loop(low, high, step, 0)

    def model(off):
        def rows(a, b):
            return jnp.concatenate([a[off : off + flat, :], b[off : off + flat, :]], axis=0)

        d_h = jnp.concatenate([drh[...], srh[...]], axis=0)
        d_l = jnp.concatenate([drl[...], srl[...]], axis=0)
        first = tdot(rows(frh, fih), jnp.concatenate([d_h, d_l], axis=1))
        second = tdot(rows(frl, fil), d_h)
        return first[:, :stations] + first[:, stations:] + second

    g_own = open_pack(0)
    g_r, g_i = g_own[:clusters], g_own[clusters:]
    xs[:clusters, :] = g_r * g_r + g_i * g_i
    tcol[...] = jnp.zeros((stations, 128), f32)
    chunks(lambda c: field_chunk(c, True), 0, 1)

    pl.semaphore_wait(barrier, n_dir + n_chan - 2)
    per = n_dir // group
    gathers = []
    for j in range(1, per):
        peer = {"dir": lax.rem(me_d + n_dir - group * j, n_dir)}
        gathers.append(send(pack.at[0], pack.at[j], gs.at[j], gr.at[j], peer))
    bands = []
    for j in range(1, n_chan):
        peer = {"chan": lax.rem(me_c + n_chan - j, n_chan)}
        bands.append(send(b_ref, b_all.at[j], bs.at[j], br.at[j], peer))
    for c in gathers + bands:
        c.start()

    count = clusters // chunk
    before = min(2, count - 1)
    for c in range(1, count):
        field_chunk(c, True)
    partial[...] = model(0)
    for c in range(before):
        power_chunk(c)

    def first_other(c):
        field_chunk(c, False)
        power_chunk(c)

    early = max(before, count - 1)
    if per > 1:
        gathers[0].wait_recv()
        open_pack(1)
        for c in range(count):
            field_chunk(c, False)
            if before <= c < early:
                power_chunk(c)
        partial[...] += model(flat)
    else:
        chunks(power_chunk, before, early)

    def others(j, carry):
        for i in range(2, per):

            @pl.when(j == i)
            def _():
                gathers[i - 1].wait_recv()

        open_pack(j)
        chunks(lambda c: field_chunk(c, False))
        partial[...] += model(flat)
        return carry

    if per > 2:
        lax.fori_loop(2, per, others, 0)
    if group == 2:
        mate = {"dir": me_d + 1 - 2 * lax.rem(me_d, 2)}
        swap = send(partial, partner, ms.at[0], mr.at[0], mate)
        swap.start()
    for c in range(early, count):
        power_chunk(c)

    row = lax.broadcasted_iota(jnp.int32, ones.shape, 0)
    col = lax.broadcasted_iota(jnp.int32, ones.shape, 1)
    ones[...] = jnp.where(lax.rem(row, clusters) == col // 128, 1.0, 0.0).astype(bf16)
    for c in loads[5:10]:
        c.wait()
    level = legendre(here)
    pen = column(pen_ref)
    pull = jnp.concatenate([pen, pen], axis=0)
    tile = 32 * NTERM
    tiles = stations // 32
    row = lax.broadcasted_iota(jnp.int32, (tile, tile), 0)
    col = lax.broadcasted_iota(jnp.int32, (tile, tile), 1)
    pick = jnp.zeros((tile, tile), f32)
    for t in range(NTERM):
        pick = jnp.where(row - NTERM * col == t, level[t], pick)
    p_h, p_l = split(pick)
    q_h, q_l = split(
        jnp.concatenate([poly[:, j * tile : (j + 1) * tile] for j in range(tiles)], axis=0)
    )
    value = dot(
        jnp.concatenate([q_h, q_l, q_h], axis=1), jnp.concatenate([p_h, p_h, p_l], axis=0)
    )
    value = jnp.concatenate(
        [value[j * rows2 : (j + 1) * rows2, :32] for j in range(tiles)], axis=1
    )
    offset[...] = halves(dual, rows2) / pull
    goal[...] = (value - offset[...]) * pull
    modes = harm.shape[1]

    def mode_block(a):
        start = lax.rem(me_d + a, n_dir) * clusters
        return harm[pl.ds(pl.multiple_of(start, clusters), clusters), :]

    mode_rows = hm.shape[0]
    turned = jnp.concatenate([mode_block(a) for a in range(n_dir)], axis=0)
    turned = jnp.concatenate(
        [turned, jnp.zeros((turned.shape[0], mode_rows - modes), f32)], axis=1
    )
    h_h, h_l = split(jnp.transpose(turned))
    hm[...] = jnp.concatenate([h_h, h_h, h_l], axis=1)
    for c in bands:
        c.wait()
    taps = fit_taps(legendre(b_all[:, 0, :]))

    loads[10].wait()
    if group == 2:
        swap.wait()
        both = partial[...] + partner[...]
    else:
        both = partial[...]
    turned = jnp.transpose(both)

    def seen(i):
        return jnp.concatenate(
            [vis[pl.ds(2 * j + i, stations, 4), :] for j in range(2)], axis=1
        )

    r_h, r_l = split(seen(0) - 0.5 * (both + turned))
    i_h, i_l = split(seen(1) - 0.5 * (both - turned))
    rs[0, :, :stations] = r_h
    rs[0, :, stations:] = -i_h
    rs[1, :, :stations] = i_h
    rs[1, :, stations:] = r_h
    rs[2, :, :stations] = r_l
    rs[2, :, stations:] = -i_l
    rs[3, :, :stations] = i_l
    rs[3, :, stations:] = r_l

    def gather_rows():
        a, b = frh[:flat, :], fih[:flat, :]
        y = dot(
            jnp.concatenate([a, b, a, b, frl[:flat, :], fil[:flat, :]], axis=1),
            jnp.concatenate([rs[0], rs[1], rs[2], rs[3], rs[0], rs[1]], axis=0),
        )
        y_r, y_i = y[:, :stations], y[:, stations:]
        e_r, e_i = er[...], ei[...]

        def over(x):
            return jnp.sum(x.reshape(clusters, sources, stations), axis=1)

        return over(e_r * y_r + e_i * y_i), over(e_r * y_i - e_i * y_r)

    n_r, n_i = gather_rows()
    total = jnp.transpose(tcol[...])[:clusters]
    inverse = 1.0 / (total + pen)
    h_r = (n_r + g_r * total + goal[:clusters, :]) * inverse
    h_i = (n_i + g_i * total + goal[clusters:, :]) * inverse
    xs[:clusters, :] = g_r * h_r + g_i * h_i
    xs[clusters:rows2, :] = g_r * h_i - g_i * h_r
    h_2 = h_r * h_r + h_i * h_i
    high = h_2.astype(bf16).astype(f32)
    two = jnp.concatenate([high, h_2 - high], axis=0)
    two = jnp.concatenate([two, jnp.zeros((128 - rows2, stations), f32)], axis=0)
    two = jnp.transpose(two)[:, :rows2].astype(bf16)
    g[:clusters, :] = h_r
    g[clusters:, :] = h_i

    def again(c):
        start = c * span
        at = pl.ds(start, span)
        f_r, f_i = times(er[at, :], ei[at, :], c, g)
        put(frh, frl, start, f_r)
        put(fih, fil, start, f_i)

    for c in range(clusters // chunk):
        again(c)
    spread_2 = dot(two, ones[...])
    m_r, m_i = gather_rows()
    for k in range(clusters):
        w = power[k]
        c = spread_2[:, 128 * k : 128 * k + 128]
        sums[2 * clusters + k : 2 * clusters + k + 1, :] = jnp.concatenate(
            [
                jnp.sum(w[:, 128 * h : 128 * h + 128] * c, axis=0, keepdims=True)
                for h in range(stations // 128)
            ],
            axis=1,
        )
        for i in range(2):
            j = i * clusters + k
            t = w * xs[j : j + 1, :]
            t = sum(t[:, 128 * h : 128 * h + 128] for h in range(1, stations // 128)) + t[:, :128]
            sums[j : j + 1, :] = jnp.sum(jnp.transpose(t), axis=0, keepdims=True)
    t_0, t_1, t_2 = (sums[i * clusters : (i + 1) * clusters, :] for i in range(3))
    inverse = 1.0 / (t_2 + pen)
    new_r = (m_r + g_r * t_0 - g_i * t_1 + goal[:clusters, :]) * inverse
    new_i = (m_i + g_r * t_1 + g_i * t_0 + goal[clusters:, :]) * inverse
    new = jnp.concatenate([new_r, new_i], axis=0)
    gains[...] = new
    emit = pltpu.make_async_copy(gains, gains_out, outs.at[0])
    emit.start()

    spread = new + offset[...]
    each = stations // n_chan
    groups = rows2 // 8
    used = groups * each
    lanes = packed.shape[2]
    for j in range(n_chan):
        if used < lanes:
            packed[j] = jnp.zeros((8, lanes), f32)
        packed[j, :, :used] = jnp.concatenate(
            [spread[8 * i : 8 * i + 8, j * each : (j + 1) * each] for i in range(groups)], axis=1
        )
    def moment(a, j):
        to_d, to_c = lax.rem(me_d + n_dir - a, n_dir), lax.rem(me_c + n_chan - j, n_chan)
        return send(
            packed.at[to_c], zin.at[a, j], s1.at[a, j], r1.at[a, j], {"dir": to_d, "chan": to_c}
        )

    everyone(lambda a, j: moment(a, j).start())
    wide = NTERM * each
    width = part.shape[1]
    rows = []
    for a in range(n_dir):
        mixed = [None] * NTERM
        for j in range(n_chan):
            if a == j == 0:
                got = packed[me_c]
            else:
                moment(a, j).wait_recv()
                got = zin[a, j]
            for t in range(NTERM):
                term = got * taps[t][j : j + 1, 0:1]
                mixed[t] = term if j == 0 else mixed[t] + term

        def terms(i):
            row = [mixed[t][:, i * each : (i + 1) * each] for t in range(NTERM)]
            if wide < width:
                row.append(jnp.zeros((8, width - wide), f32))
            return jnp.concatenate(row, axis=1)

        tall = groups // 2
        rows.append(
            jnp.concatenate(
                [
                    jnp.concatenate([terms(r * tall + i) for i in range(tall)], axis=0)
                    for r in range(2)
                ],
                axis=1,
            )
        )
    z_h, z_l = split(jnp.concatenate(rows, axis=0))
    a = dot(hm[...], jnp.concatenate([z_h, z_l, z_h], axis=0))
    a_r, a_i = a[:, :width], a[:, width:]
    size = jnp.sqrt(a_r * a_r + a_i * a_i)
    limit = cut[0]
    scale = jnp.maximum(size - limit, 0.0) / jnp.maximum(size, limit)
    a_h, a_l = split(jnp.concatenate([a_r * scale, a_i * scale], axis=1)[:modes])
    m_h, m_l = split(mode_block(0))
    twice = dot(jnp.concatenate([m_h, m_l], axis=0), a_h)
    done = twice[:clusters] + twice[clusters:] + dot(m_h, a_l)
    part[:clusters] = done[:, :width]
    part[clusters:] = done[:, width:]
    third = []
    for j in range(1, n_chan):
        peer = lax.rem(me_c + j, n_chan)
        third.append(send(part, blocks.at[me_c], s3.at[j], r3.at[j], {"chan": peer}))
    for c in third:
        c.start()
    keep = pltpu.make_async_copy(part, blocks.at[me_c], outs.at[1])
    keep.start()
    show = pltpu.make_async_copy(b_ref, band_out, outs.at[2])
    show.start()
    for c in gathers:
        c.wait_send()
    everyone(lambda a, j: moment(a, j).wait_send())
    emit.wait()
    keep.wait()
    show.wait()
    for c in third:
        c.wait()


def emit_kernel(blocks, gains, dual, pen_ref, band, gains_out, dual_out, cons_out):
    n_chan, rows2, width = blocks.shape
    stations = gains.shape[1]
    each = stations // n_chan
    wide = NTERM * each
    level = legendre(band[0:1, 0:1])
    row = lax.broadcasted_iota(jnp.int32, (width, width), 0)
    col = lax.broadcasted_iota(jnp.int32, (width, width), 1)
    weave = jnp.zeros((width, width), f32)
    sample = jnp.zeros((width, width), f32)
    for t in range(NTERM):
        place = row - t * each
        inside = (place >= 0) & (place < each)
        weave = jnp.where(inside & (col == NTERM * place + t), 1.0, weave)
        sample = jnp.where(inside & (col == place), level[t], sample)
    s_h, s_l = split(sample)
    both = jnp.concatenate([weave.astype(bf16), s_h], axis=1)
    rest = jnp.concatenate([jnp.zeros((width, width), bf16), s_l], axis=1)
    b_h, b_l = split(jnp.concatenate([blocks[j] for j in range(n_chan)], axis=0))
    result = dot(
        jnp.concatenate([b_h, b_l, b_h], axis=1), jnp.concatenate([both, both, rest], axis=0)
    )
    fitted = []
    for j in range(n_chan):
        piece = result[j * rows2 : (j + 1) * rows2]
        cons_out[:, j * wide : (j + 1) * wide] = piece[:, :wide]
        fitted.append(piece[:, width : width + each])
    fitted = jnp.concatenate(fitted, axis=1)
    pen = column(pen_ref)
    pull = jnp.concatenate([pen, pen], axis=0)
    new = gains[...]
    fresh = halves(dual, rows2) + pull * (new - fitted)
    for j in range(2):
        gains_out[pl.ds(j, rows2, 2), :] = new[:, j * 128 : (j + 1) * 128]
        dual_out[pl.ds(j, rows2, 2), :] = fresh[:, j * 128 : (j + 1) * 128]


def solution(mesh):
    n_dir, n_chan = mesh.shape["dir"], mesh.shape["chan"]
    group = 2 if n_dir % 2 == 0 else 1

    def shards(
        visibilities, station_uv, source_lm, source_flux, band_offset, gains_init, duals_init,
        poly_init, penalty, harmonics, threshold,
    ):
        _, clusters, sources = source_lm.shape
        stations = station_uv.shape[1]
        modes = harmonics.shape[1]
        mode_rows = -(-modes // 128) * 128
        rows2 = 2 * clusters
        lanes = max(128, stations * NTERM // n_chan)
        flat = clusters * sources
        small = max(128, stations // n_chan * (rows2 // 8))
        vis = visibilities.reshape(stations, 2, stations // 128, 128)
        vis = vis.transpose(0, 2, 1, 3).reshape(stations * 4, 128)
        lines = rows2 * stations // 128
        dual = duals_init.reshape(lines, 128)
        pen = penalty.reshape(1, clusters)
        dma = pltpu.SemaphoreType.DMA
        vm = pltpu.VMEM
        wide16 = vm((flat, stations), bf16)
        long16 = vm((2 * flat, stations), bf16)
        per = n_dir // group
        gains, blocks, band = pl.pallas_call(
            functools.partial(step_kernel, n_dir, n_chan, group),
            out_shape=(
                jax.ShapeDtypeStruct((rows2, stations), f32),
                jax.ShapeDtypeStruct((n_chan, rows2, lanes), f32),
                jax.ShapeDtypeStruct((8, 128), f32),
            ),
            in_specs=[ANY] * 11,
            out_specs=(ANY,) * 3,
            scratch_shapes=[
                vm((stations * 4, 128), f32),
                vm(station_uv.shape, f32),
                vm(source_lm.shape, f32),
                vm(source_flux.shape, f32),
                pltpu.SMEM((1,), f32),
                vm((lines, 128), f32),
                vm((rows2, stations * NTERM), f32),
                vm(pen.shape, f32),
                vm(harmonics.shape, f32),
                pltpu.SMEM((1,), f32),
                vm((8, 128), f32),
                vm((n_chan, 8, 128), f32),
                vm((per, lines + sources, 128), f32),
                vm((flat, 128), f32),
                vm((rows2, stations), f32),
                vm((flat, stations), f32),
                vm((flat, stations), f32),
                wide16, wide16, wide16, wide16, wide16, wide16,
                long16, long16, long16, long16,
                wide16, wide16, wide16, wide16,
                vm((stations, stations), f32),
                vm((stations, stations), f32),
                vm((4, stations, 2 * stations), bf16),
                vm((clusters, stations, stations), f32),
                vm((rows2, clusters * 128), bf16),
                vm((rows2, stations), f32),
                vm((3 * clusters, stations), f32),
                vm((stations, 128), f32),
                vm((rows2, stations), f32),
                vm((rows2, stations), f32),
                vm((mode_rows, 3 * harmonics.shape[0]), bf16),
                vm((n_chan, 8, small), f32),
                vm((n_dir, n_chan, 8, small), f32),
                vm((rows2, lanes), f32),
                vm((rows2, stations), f32),
                dma((11,)),
                dma((per,)), dma((per,)),
                dma((1,)), dma((1,)),
                dma((n_chan,)), dma((n_chan,)),
                dma((n_dir, n_chan)), dma((n_dir, n_chan)),
                dma((n_chan,)), dma((n_chan,)),
                dma((3,)),
            ],
            compiler_params=pltpu.CompilerParams(
                collective_id=0, has_side_effects=True, vmem_limit_bytes=62 * 2**20
            ),
            name="calibrate",
        )(
            vis, station_uv, source_lm, source_flux, band_offset, gains_init.reshape(lines, 128), dual,
            poly_init.reshape(rows2, stations * NTERM), pen, harmonics, threshold,
        )
        gains, duals, consensus = pl.pallas_call(
            emit_kernel,
            out_shape=(
                jax.ShapeDtypeStruct((lines, 128), f32),
                jax.ShapeDtypeStruct((lines, 128), f32),
                jax.ShapeDtypeStruct((rows2, stations * NTERM), f32),
            ),
            in_specs=[VM] * 5,
            out_specs=(VM,) * 3,
            name="emit",
        )(blocks, gains, dual, pen, band)
        shape = (2, clusters, 1, stations)
        return (
            gains.reshape(shape),
            duals.reshape(shape),
            consensus.reshape(2, clusters, stations * NTERM),
        )

    return jax.shard_map(
        shards,
        mesh=mesh,
        in_specs=(
            P("chan", None, None, None),
            P(),
            P(None, "dir", None),
            P("dir", None),
            P("chan"),
            P(None, "dir", "chan", None),
            P(None, "dir", "chan", None),
            P(None, "dir", None),
            P("dir"),
            P(),
            P(),
        ),
        out_specs=(
            P(None, "dir", "chan", None),
            P(None, "dir", "chan", None),
            P(None, "dir", None),
        ),
        check_vma=False,
    )
```

```python
import functools

import jax
import jax.numpy as jnp
import numpy as np
from jax import lax
from jax.experimental import pallas as pl
from jax.experimental.pallas import tpu as pltpu
from jax.sharding import PartitionSpec as P

NTERM = 4
MESH = pl.DeviceIdType.MESH
VM = pl.BlockSpec(memory_space=pltpu.VMEM)
ANY = pl.BlockSpec(memory_space=pltpu.HBM)
f32, bf16 = jnp.float32, jnp.bfloat16


def fit_half_circle():
    nodes = np.cos(np.pi * (np.arange(400) + 0.5) / 800.0) * 0.5
    square = nodes * nodes
    fit = np.polynomial.chebyshev.Chebyshev.fit
    root = np.sqrt(2.0)
    sine = fit(square, root * np.sin(np.pi * nodes) / nodes, 3, domain=[0, 0.25], w=nodes)
    cosine = fit(square, root * np.cos(np.pi * nodes), 4, domain=[0, 0.25])
    kind = np.polynomial.Polynomial
    return [[float(c) for c in p.convert(kind=kind).coef] for p in (sine, cosine)]


SINE, COSINE = fit_half_circle()


def horner(coefs, x):
    total = coefs[-1] * x + coefs[-2]
    for c in coefs[-3::-1]:
        total = total * x + c
    return total


def legendre(x):
    return [
        jnp.ones_like(x),
        x,
        0.5 * (3.0 * x * x - 1.0),
        0.5 * (5.0 * x * x * x - 3.0 * x),
    ]


def split(x):
    high = x.astype(bf16)
    low = (x - high.astype(f32)).astype(bf16)
    return high, low


def dot(a, b):
    return jnp.dot(a, b, preferred_element_type=f32)


def tdot(a, b):
    return lax.dot_general(a, b, (((0,), (0,)), ((), ())), preferred_element_type=f32)


def column(pen):
    count = pen.shape[1]
    row = lax.broadcasted_iota(jnp.int32, (count, count), 0)
    col = lax.broadcasted_iota(jnp.int32, (count, count), 1)
    return jnp.sum(jnp.where(row == col, pen[...], 0.0), axis=1, keepdims=True)


def halves(ref, rows):
    return jnp.concatenate([ref[pl.ds(j, rows, 2), :] for j in range(2)], axis=1)


def fit_taps(values):
    gram = [
        [jnp.sum(values[t] * values[s], axis=0, keepdims=True) for s in range(t + 1)]
        for t in range(NTERM)
    ]
    factor = [[None] * NTERM for _ in range(NTERM)]
    for t in range(NTERM):
        for s in range(t + 1):
            rest = gram[t][s]
            for r in range(s):
                rest = rest - factor[t][r] * factor[s][r]
            factor[t][s] = jnp.sqrt(rest) if s == t else rest / factor[s][s]
    half = []
    for t in range(NTERM):
        rest = values[t]
        for s in range(t):
            rest = rest - factor[t][s] * half[s]
        half.append(rest / factor[t][t])
    taps = [None] * NTERM
    for t in reversed(range(NTERM)):
        rest = half[t]
        for s in range(t + 1, NTERM):
            rest = rest - factor[s][t] * taps[s]
        taps[t] = rest / factor[t][t]
    return taps


def step_kernel(
    n_dir, n_chan, group,
    vis_hbm, uv_hbm, lm_hbm, flux_hbm, band_hbm, g_hbm, dual_hbm, poly_hbm, pen_hbm, harm_hbm,
    cut_hbm,
    gains_out, blocks, band_out,
    vis, uv, lm, flux, band, dual, poly, pen_ref, harm, cut,
    b_ref, b_all, pack, src, g, er, ei,
    erh, erl, eih, eil, nih, nil,
    frh, frl, fih, fil, drh, drl, srh, srl,
    partial, partner,
    rs, power, ones, xs, sums, tcol, goal, offset, hm,
    packed, zin, part, gains,
    ins, gs, gr, ms, mr, bs, br, s1, r1, s3, r3, outs,
):
    rows2, stations = g.shape
    clusters = rows2 // 2
    sources = er.shape[0] // clusters
    flat = clusters * sources
    me_d, me_c = lax.axis_index("dir"), lax.axis_index("chan")
    barrier = pltpu.get_barrier_semaphore()
    members = n_dir * n_chan

    def everyone(body):
        if members <= 64:
            for i in range(1, members):
                body(i // n_chan, i % n_chan)
        else:

            def step(i, carry):
                body(i // n_chan, i % n_chan)
                return carry

            lax.fori_loop(1, members, step, 0)

    for j in range(1, n_dir):
        pl.semaphore_signal(
            barrier, inc=1, device_id={"dir": lax.rem(me_d + j, n_dir)}, device_id_type=MESH
        )
    for j in range(1, n_chan):
        pl.semaphore_signal(
            barrier, inc=1, device_id={"chan": lax.rem(me_c + j, n_chan)}, device_id_type=MESH
        )
    loads = [
        pltpu.make_async_copy(a, b, ins.at[i])
        for i, (a, b) in enumerate(
            [
                (band_hbm, band),
                (lm_hbm, lm),
                (flux_hbm, flux),
                (g_hbm, pack.at[0, : 4 * clusters]),
                (uv_hbm, uv),
                (cut_hbm, cut),
                (dual_hbm, dual),
                (poly_hbm, poly),
                (pen_hbm, pen_ref),
                (harm_hbm, harm),
                (vis_hbm, vis),
            ]
        )
    ]
    for c in loads:
        c.start()

    def send(s, d, a, b, peer):
        return pltpu.make_async_remote_copy(
            src_ref=s, dst_ref=d, send_sem=a, recv_sem=b, device_id=peer, device_id_type=MESH
        )

    for c in loads[:5]:
        c.wait()
    table = jnp.concatenate([lm[0], lm[1], jnp.sqrt(flux[...])], axis=0)
    fill = (-3 * clusters) % 128
    table = jnp.concatenate([table, jnp.zeros((fill, sources), f32)], axis=0)
    pack[0, 4 * clusters : 4 * clusters + sources, :] = jnp.transpose(table)
    here = jnp.full((1, 1), band[0], f32)
    b_ref[...] = jnp.full(b_ref.shape, band[0], f32)
    b_all[0] = b_ref[...]
    stretch = 1.0 + 0.25 * here
    u = uv[0:1, :] * stretch
    v = uv[1:2, :] * stretch

    def open_pack(slot):
        g_all = halves(pack.at[slot, : 4 * clusters], rows2)
        g[...] = g_all
        t = pack[slot, 4 * clusters : 4 * clusters + sources, :]
        for k in range(clusters):
            src[k * sources : (k + 1) * sources, :] = pltpu.roll(t, (128 - k) % 128, 1)
        return g_all

    chunk = 4
    span = chunk * sources

    def circle(start):
        cols = src[pl.ds(start, span), :]
        turns = cols[:, 0:1] * u + cols[:, clusters : clusters + 1] * v
        r = turns - jnp.round(turns)
        square = r * r
        s = r * horner(SINE, square)
        c = horner(COSINE, square)
        w = cols[:, 2 * clusters : 2 * clusters + 1]
        ws = w * s
        return w - ws * s, ws * c

    def times(e_r, e_i, c, ref):
        f_r, f_i = [], []
        for i in range(chunk):
            a = ref[pl.ds(c * chunk + i, 1), :]
            b = ref[pl.ds(clusters + c * chunk + i, 1), :]
            p_r = e_r[i * sources : (i + 1) * sources]
            p_i = e_i[i * sources : (i + 1) * sources]
            f_r.append(p_r * a - p_i * b)
            f_i.append(p_r * b + p_i * a)
        return jnp.concatenate(f_r, axis=0), jnp.concatenate(f_i, axis=0)

    def put(h_ref, l_ref, start, x):
        h, l = split(x)
        h_ref[pl.ds(start, span), :] = h
        l_ref[pl.ds(start, span), :] = l
        return h, l

    def field_chunk(c, keep):
        start = c * span if isinstance(c, int) else pl.multiple_of(c * span, span)
        e_r, e_i = circle(start)
        if keep:
            er[pl.ds(start, span), :] = e_r
            ei[pl.ds(start, span), :] = e_i
            put(erh, erl, start, e_r)
            h, l = put(eih, eil, start, e_i)
            nih[pl.ds(start, span), :] = -h
            nil[pl.ds(start, span), :] = -l
        f_r, f_i = times(e_r, e_i, c, g)
        off = 0 if keep else flat
        put(frh, frl, start + off, f_r)
        put(fih, fil, start + off, f_i)
        put(drh, drl, start, f_r - f_i)
        put(srh, srl, start, f_i + f_r)

    lane = lax.broadcasted_iota(jnp.int32, (stations, 128), 1)

    def power_chunk(c):
        acc = tcol[...]
        for i in range(chunk):
            k = c * chunk + i
            at = k * sources
            at = pl.ds(at if isinstance(k, int) else pl.multiple_of(at, sources), sources)
            r_h, r_l, i_h, i_l = erh[at, :], erl[at, :], eih[at, :], eil[at, :]
            n_h, n_l = nih[at, :], nil[at, :]
            left = jnp.concatenate([r_h, i_h, r_h, i_h, r_l, i_l], axis=0)
            real = jnp.concatenate([r_h, i_h, r_l, i_l, r_h, i_h], axis=0)
            imag = jnp.concatenate([n_h, r_h, n_l, r_l, n_h, r_h], axis=0)
            both = tdot(left, jnp.concatenate([real, imag], axis=1))
            c_r, c_i = both[:, :stations], both[:, stations:]
            w = c_r * c_r + c_i * c_i
            power[k] = w
            t = jnp.sum(w * xs[pl.ds(k, 1), :], axis=1, keepdims=True)
            acc = jnp.where(lane == k, t, acc)
        tcol[...] = acc

    def chunks(body, low=0, high=clusters // chunk):
        def step(c, carry):
            body(c)
            return carry

        lax.fori_loop(low, high, step, 0)

    def model(off):
        def rows(a, b):
            return jnp.concatenate([a[off : off + flat, :], b[off : off + flat, :]], axis=0)

        d_h = jnp.concatenate([drh[...], srh[...]], axis=0)
        d_l = jnp.concatenate([drl[...], srl[...]], axis=0)
        first = tdot(rows(frh, fih), jnp.concatenate([d_h, d_l], axis=1))
        second = tdot(rows(frl, fil), d_h)
        return first[:, :stations] + first[:, stations:] + second

    g_own = open_pack(0)
    g_r, g_i = g_own[:clusters], g_own[clusters:]
    xs[:clusters, :] = g_r * g_r + g_i * g_i
    tcol[...] = jnp.zeros((stations, 128), f32)
    chunks(lambda c: field_chunk(c, True), 0, 1)

    pl.semaphore_wait(barrier, n_dir + n_chan - 2)
    per = n_dir // group
    gathers = []
    for j in range(1, per):
        peer = {"dir": lax.rem(me_d + n_dir - group * j, n_dir)}
        gathers.append(send(pack.at[0], pack.at[j], gs.at[j], gr.at[j], peer))
    bands = []
    for j in range(1, n_chan):
        peer = {"chan": lax.rem(me_c + n_chan - j, n_chan)}
        bands.append(send(b_ref, b_all.at[j], bs.at[j], br.at[j], peer))
    for c in gathers + bands:
        c.start()

    count = clusters // chunk
    before = min(3, count - 1)
    for c in range(1, count):
        field_chunk(c, True)
    partial[...] = model(0)
    for c in range(before):
        power_chunk(c)

    def first_other(c):
        field_chunk(c, False)
        power_chunk(c)

    early = max(before, count - 1)
    if per > 1:
        gathers[0].wait_recv()
        open_pack(1)
        for c in range(count):
            field_chunk(c, False)
            if before <= c < early:
                power_chunk(c)
        partial[...] += model(flat)
    else:
        chunks(power_chunk, before, early)

    def others(j, carry):
        for i in range(2, per):

            @pl.when(j == i)
            def _():
                gathers[i - 1].wait_recv()

        open_pack(j)
        chunks(lambda c: field_chunk(c, False))
        partial[...] += model(flat)
        return carry

    if per > 2:
        lax.fori_loop(2, per, others, 0)
    if group == 2:
        mate = {"dir": me_d + 1 - 2 * lax.rem(me_d, 2)}
        swap = send(partial, partner, ms.at[0], mr.at[0], mate)
        swap.start()
    for c in range(early, count):
        power_chunk(c)

    row = lax.broadcasted_iota(jnp.int32, ones.shape, 0)
    col = lax.broadcasted_iota(jnp.int32, ones.shape, 1)
    ones[...] = jnp.where(lax.rem(row, clusters) == col // 128, 1.0, 0.0).astype(bf16)
    for c in loads[5:10]:
        c.wait()
    level = legendre(here)
    pen = column(pen_ref)
    pull = jnp.concatenate([pen, pen], axis=0)
    tile = 32 * NTERM
    tiles = stations // 32
    row = lax.broadcasted_iota(jnp.int32, (tile, tile), 0)
    col = lax.broadcasted_iota(jnp.int32, (tile, tile), 1)
    pick = jnp.zeros((tile, tile), f32)
    for t in range(NTERM):
        pick = jnp.where(row - NTERM * col == t, level[t], pick)
    p_h, p_l = split(pick)
    q_h, q_l = split(
        jnp.concatenate([poly[:, j * tile : (j + 1) * tile] for j in range(tiles)], axis=0)
    )
    value = dot(
        jnp.concatenate([q_h, q_l, q_h], axis=1), jnp.concatenate([p_h, p_h, p_l], axis=0)
    )
    value = jnp.concatenate(
        [value[j * rows2 : (j + 1) * rows2, :32] for j in range(tiles)], axis=1
    )
    offset[...] = halves(dual, rows2) / pull
    goal[...] = (value - offset[...]) * pull
    modes = harm.shape[1]

    def mode_block(a):
        start = lax.rem(me_d + a, n_dir) * clusters
        return harm[pl.ds(pl.multiple_of(start, clusters), clusters), :]

    mode_rows = hm.shape[0]
    turned = jnp.concatenate([mode_block(a) for a in range(n_dir)], axis=0)
    turned = jnp.concatenate(
        [turned, jnp.zeros((turned.shape[0], mode_rows - modes), f32)], axis=1
    )
    h_h, h_l = split(jnp.transpose(turned))
    hm[...] = jnp.concatenate([h_h, h_h, h_l], axis=1)
    for c in bands:
        c.wait()
    taps = fit_taps(legendre(b_all[:, 0, :]))

    loads[10].wait()
    if group == 2:
        swap.wait()
        both = partial[...] + partner[...]
    else:
        both = partial[...]
    turned = jnp.transpose(both)

    def seen(i):
        return jnp.concatenate(
            [vis[pl.ds(2 * j + i, stations, 4), :] for j in range(2)], axis=1
        )

    r_h, r_l = split(seen(0) - 0.5 * (both + turned))
    i_h, i_l = split(seen(1) - 0.5 * (both - turned))
    rs[0, :, :stations] = r_h
    rs[0, :, stations:] = -i_h
    rs[1, :, :stations] = i_h
    rs[1, :, stations:] = r_h
    rs[2, :, :stations] = r_l
    rs[2, :, stations:] = -i_l
    rs[3, :, :stations] = i_l
    rs[3, :, stations:] = r_l

    def gather_rows():
        a, b = frh[:flat, :], fih[:flat, :]
        y = dot(
            jnp.concatenate([a, b, a, b, frl[:flat, :], fil[:flat, :]], axis=1),
            jnp.concatenate([rs[0], rs[1], rs[2], rs[3], rs[0], rs[1]], axis=0),
        )
        y_r, y_i = y[:, :stations], y[:, stations:]
        e_r, e_i = er[...], ei[...]

        def over(x):
            return jnp.sum(x.reshape(clusters, sources, stations), axis=1)

        return over(e_r * y_r + e_i * y_i), over(e_r * y_i - e_i * y_r)

    n_r, n_i = gather_rows()
    total = jnp.transpose(tcol[...])[:clusters]
    inverse = 1.0 / (total + pen)
    h_r = (n_r + g_r * total + goal[:clusters, :]) * inverse
    h_i = (n_i + g_i * total + goal[clusters:, :]) * inverse
    xs[:clusters, :] = g_r * h_r + g_i * h_i
    xs[clusters:rows2, :] = g_r * h_i - g_i * h_r
    h_2 = h_r * h_r + h_i * h_i
    high = h_2.astype(bf16).astype(f32)
    two = jnp.concatenate([high, h_2 - high], axis=0)
    two = jnp.concatenate([two, jnp.zeros((128 - rows2, stations), f32)], axis=0)
    two = jnp.transpose(two)[:, :rows2].astype(bf16)
    g[:clusters, :] = h_r
    g[clusters:, :] = h_i

    def again(c):
        start = c * span
        at = pl.ds(start, span)
        f_r, f_i = times(er[at, :], ei[at, :], c, g)
        put(frh, frl, start, f_r)
        put(fih, fil, start, f_i)

    for c in range(clusters // chunk):
        again(c)
    spread_2 = dot(two, ones[...])
    m_r, m_i = gather_rows()
    for k in range(clusters):
        w = power[k]
        c = spread_2[:, 128 * k : 128 * k + 128]
        sums[2 * clusters + k : 2 * clusters + k + 1, :] = jnp.concatenate(
            [
                jnp.sum(w[:, 128 * h : 128 * h + 128] * c, axis=0, keepdims=True)
                for h in range(stations // 128)
            ],
            axis=1,
        )
        for i in range(2):
            j = i * clusters + k
            t = w * xs[j : j + 1, :]
            t = sum(t[:, 128 * h : 128 * h + 128] for h in range(1, stations // 128)) + t[:, :128]
            sums[j : j + 1, :] = jnp.sum(jnp.transpose(t), axis=0, keepdims=True)
    t_0, t_1, t_2 = (sums[i * clusters : (i + 1) * clusters, :] for i in range(3))
    inverse = 1.0 / (t_2 + pen)
    new_r = (m_r + g_r * t_0 - g_i * t_1 + goal[:clusters, :]) * inverse
    new_i = (m_i + g_r * t_1 + g_i * t_0 + goal[clusters:, :]) * inverse
    new = jnp.concatenate([new_r, new_i], axis=0)
    gains[...] = new
    emit = pltpu.make_async_copy(gains, gains_out, outs.at[0])
    emit.start()

    spread = new + offset[...]
    each = stations // n_chan
    groups = rows2 // 8
    used = groups * each
    lanes = packed.shape[2]
    for j in range(n_chan):
        if used < lanes:
            packed[j] = jnp.zeros((8, lanes), f32)
        packed[j, :, :used] = jnp.concatenate(
            [spread[8 * i : 8 * i + 8, j * each : (j + 1) * each] for i in range(groups)], axis=1
        )
    def moment(a, j):
        to_d, to_c = lax.rem(me_d + n_dir - a, n_dir), lax.rem(me_c + n_chan - j, n_chan)
        return send(
            packed.at[to_c], zin.at[a, j], s1.at[a, j], r1.at[a, j], {"dir": to_d, "chan": to_c}
        )

    everyone(lambda a, j: moment(a, j).start())
    wide = NTERM * each
    width = part.shape[1]
    rows = []
    for a in range(n_dir):
        mixed = [None] * NTERM
        for j in range(n_chan):
            if a == j == 0:
                got = packed[me_c]
            else:
                moment(a, j).wait_recv()
                got = zin[a, j]
            for t in range(NTERM):
                term = got * taps[t][j : j + 1, 0:1]
                mixed[t] = term if j == 0 else mixed[t] + term

        def terms(i):
            row = [mixed[t][:, i * each : (i + 1) * each] for t in range(NTERM)]
            if wide < width:
                row.append(jnp.zeros((8, width - wide), f32))
            return jnp.concatenate(row, axis=1)

        tall = groups // 2
        rows.append(
            jnp.concatenate(
                [
                    jnp.concatenate([terms(r * tall + i) for i in range(tall)], axis=0)
                    for r in range(2)
                ],
                axis=1,
            )
        )
    z_h, z_l = split(jnp.concatenate(rows, axis=0))
    a = dot(hm[...], jnp.concatenate([z_h, z_l, z_h], axis=0))
    a_r, a_i = a[:, :width], a[:, width:]
    size = jnp.sqrt(a_r * a_r + a_i * a_i)
    limit = cut[0]
    scale = jnp.maximum(size - limit, 0.0) / jnp.maximum(size, limit)
    a_h, a_l = split(jnp.concatenate([a_r * scale, a_i * scale], axis=1)[:modes])
    m_h, m_l = split(mode_block(0))
    twice = dot(jnp.concatenate([m_h, m_l], axis=0), a_h)
    done = twice[:clusters] + twice[clusters:] + dot(m_h, a_l)
    part[:clusters] = done[:, :width]
    part[clusters:] = done[:, width:]
    third = []
    for j in range(1, n_chan):
        peer = lax.rem(me_c + j, n_chan)
        third.append(send(part, blocks.at[me_c], s3.at[j], r3.at[j], {"chan": peer}))
    for c in third:
        c.start()
    keep = pltpu.make_async_copy(part, blocks.at[me_c], outs.at[1])
    keep.start()
    show = pltpu.make_async_copy(b_ref, band_out, outs.at[2])
    show.start()
    for c in gathers:
        c.wait_send()
    everyone(lambda a, j: moment(a, j).wait_send())
    emit.wait()
    keep.wait()
    show.wait()
    for c in third:
        c.wait()


def emit_kernel(
    blocks_hbm, gains_hbm, dual_hbm, pen_hbm, band_hbm, gains_hbm_out, dual_hbm_out, cons_hbm_out,
    blocks, gains, dual, pen_ref, band, gains_out, dual_out, cons_out, ins, outs,
):
    pairs = [
        (blocks_hbm, blocks), (band_hbm, band), (gains_hbm, gains), (dual_hbm, dual),
        (pen_hbm, pen_ref),
    ]
    loads = [pltpu.make_async_copy(x, y, ins.at[i]) for i, (x, y) in enumerate(pairs)]
    for c in loads:
        c.start()
    pairs = [(gains_out, gains_hbm_out), (cons_out, cons_hbm_out), (dual_out, dual_hbm_out)]
    stores = [pltpu.make_async_copy(x, y, outs.at[i]) for i, (x, y) in enumerate(pairs)]
    n_chan, rows2, width = blocks.shape
    stations = gains.shape[1]
    each = stations // n_chan
    wide = NTERM * each
    loads[1].wait()
    level = legendre(band[0:1, 0:1])
    row = lax.broadcasted_iota(jnp.int32, (width, width), 0)
    col = lax.broadcasted_iota(jnp.int32, (width, width), 1)
    weave = jnp.zeros((width, width), f32)
    sample = jnp.zeros((width, width), f32)
    for t in range(NTERM):
        place = row - t * each
        inside = (place >= 0) & (place < each)
        weave = jnp.where(inside & (col == NTERM * place + t), 1.0, weave)
        sample = jnp.where(inside & (col == place), level[t], sample)
    s_h, s_l = split(sample)
    both = jnp.concatenate([weave.astype(bf16), s_h], axis=1)
    rest = jnp.concatenate([jnp.zeros((width, width), bf16), s_l], axis=1)
    for c in loads[2:] + loads[:1]:
        c.wait()
    pen = column(pen_ref)
    pull = jnp.concatenate([pen, pen], axis=0)
    new = gains[...]
    for j in range(2):
        gains_out[pl.ds(j, rows2, 2), :] = new[:, j * 128 : (j + 1) * 128]
    stores[0].start()
    b_h, b_l = split(jnp.concatenate([blocks[j] for j in range(n_chan)], axis=0))
    result = dot(
        jnp.concatenate([b_h, b_l, b_h], axis=1), jnp.concatenate([both, both, rest], axis=0)
    )
    fitted = []
    for j in range(n_chan):
        piece = result[j * rows2 : (j + 1) * rows2]
        cons_out[:, j * wide : (j + 1) * wide] = piece[:, :wide]
        fitted.append(piece[:, width : width + each])
    stores[1].start()
    fitted = jnp.concatenate(fitted, axis=1)
    fresh = halves(dual, rows2) + pull * (new - fitted)
    for j in range(2):
        dual_out[pl.ds(j, rows2, 2), :] = fresh[:, j * 128 : (j + 1) * 128]
    stores[2].start()
    for c in stores:
        c.wait()


def solution(mesh):
    n_dir, n_chan = mesh.shape["dir"], mesh.shape["chan"]
    group = 2 if n_dir % 2 == 0 else 1

    def shards(
        visibilities, station_uv, source_lm, source_flux, band_offset, gains_init, duals_init,
        poly_init, penalty, harmonics, threshold,
    ):
        _, clusters, sources = source_lm.shape
        stations = station_uv.shape[1]
        modes = harmonics.shape[1]
        mode_rows = -(-modes // 128) * 128
        rows2 = 2 * clusters
        lanes = max(128, stations * NTERM // n_chan)
        flat = clusters * sources
        small = max(128, stations // n_chan * (rows2 // 8))
        vis = visibilities.reshape(stations, 2, stations // 128, 128)
        vis = vis.transpose(0, 2, 1, 3).reshape(stations * 4, 128)
        lines = rows2 * stations // 128
        dual = duals_init.reshape(lines, 128)
        pen = penalty.reshape(1, clusters)
        dma = pltpu.SemaphoreType.DMA
        vm = pltpu.VMEM
        wide16 = vm((flat, stations), bf16)
        long16 = vm((2 * flat, stations), bf16)
        per = n_dir // group
        gains, blocks, band = pl.pallas_call(
            functools.partial(step_kernel, n_dir, n_chan, group),
            out_shape=(
                jax.ShapeDtypeStruct((rows2, stations), f32),
                jax.ShapeDtypeStruct((n_chan, rows2, lanes), f32),
                jax.ShapeDtypeStruct((8, 128), f32),
            ),
            in_specs=[ANY] * 11,
            out_specs=(ANY,) * 3,
            scratch_shapes=[
                vm((stations * 4, 128), f32),
                vm(station_uv.shape, f32),
                vm(source_lm.shape, f32),
                vm(source_flux.shape, f32),
                pltpu.SMEM((1,), f32),
                vm((lines, 128), f32),
                vm((rows2, stations * NTERM), f32),
                vm(pen.shape, f32),
                vm(harmonics.shape, f32),
                pltpu.SMEM((1,), f32),
                vm((8, 128), f32),
                vm((n_chan, 8, 128), f32),
                vm((per, lines + sources, 128), f32),
                vm((flat, 128), f32),
                vm((rows2, stations), f32),
                vm((flat, stations), f32),
                vm((flat, stations), f32),
                wide16, wide16, wide16, wide16, wide16, wide16,
                long16, long16, long16, long16,
                wide16, wide16, wide16, wide16,
                vm((stations, stations), f32),
                vm((stations, stations), f32),
                vm((4, stations, 2 * stations), bf16),
                vm((clusters, stations, stations), f32),
                vm((rows2, clusters * 128), bf16),
                vm((rows2, stations), f32),
                vm((3 * clusters, stations), f32),
                vm((stations, 128), f32),
                vm((rows2, stations), f32),
                vm((rows2, stations), f32),
                vm((mode_rows, 3 * harmonics.shape[0]), bf16),
                vm((n_chan, 8, small), f32),
                vm((n_dir, n_chan, 8, small), f32),
                vm((rows2, lanes), f32),
                vm((rows2, stations), f32),
                dma((11,)),
                dma((per,)), dma((per,)),
                dma((1,)), dma((1,)),
                dma((n_chan,)), dma((n_chan,)),
                dma((n_dir, n_chan)), dma((n_dir, n_chan)),
                dma((n_chan,)), dma((n_chan,)),
                dma((3,)),
            ],
            compiler_params=pltpu.CompilerParams(
                collective_id=0, has_side_effects=True, vmem_limit_bytes=62 * 2**20
            ),
            name="calibrate",
        )(
            vis, station_uv, source_lm, source_flux, band_offset, gains_init.reshape(lines, 128), dual,
            poly_init.reshape(rows2, stations * NTERM), pen, harmonics, threshold,
        )
        gains, duals, consensus = pl.pallas_call(
            emit_kernel,
            out_shape=(
                jax.ShapeDtypeStruct((lines, 128), f32),
                jax.ShapeDtypeStruct((lines, 128), f32),
                jax.ShapeDtypeStruct((rows2, stations * NTERM), f32),
            ),
            in_specs=[ANY] * 5,
            out_specs=(ANY,) * 3,
            scratch_shapes=[
                vm((n_chan, rows2, lanes), f32),
                vm((rows2, stations), f32),
                vm((lines, 128), f32),
                vm(pen.shape, f32),
                vm((8, 128), f32),
                vm((lines, 128), f32),
                vm((lines, 128), f32),
                vm((rows2, stations * NTERM), f32),
                dma((5,)),
                dma((3,)),
            ],
            compiler_params=pltpu.CompilerParams(vmem_limit_bytes=62 * 2**20),
            name="emit",
        )(blocks, gains, dual, pen, band)
        shape = (2, clusters, 1, stations)
        return (
            gains.reshape(shape),
            duals.reshape(shape),
            consensus.reshape(2, clusters, stations * NTERM),
        )

    return jax.shard_map(
        shards,
        mesh=mesh,
        in_specs=(
            P("chan", None, None, None),
            P(),
            P(None, "dir", None),
            P("dir", None),
            P("chan"),
            P(None, "dir", "chan", None),
            P(None, "dir", "chan", None),
            P(None, "dir", None),
            P("dir"),
            P(),
            P(),
        ),
        out_specs=(
            P(None, "dir", "chan", None),
            P(None, "dir", "chan", None),
            P(None, "dir", None),
        ),
        check_vma=False,
    )
```

```python
import functools

import jax
import jax.numpy as jnp
import numpy as np
from jax import lax
from jax.experimental import pallas as pl
from jax.experimental.pallas import tpu as pltpu
from jax.sharding import PartitionSpec as P

NTERM = 4
MESH = pl.DeviceIdType.MESH
VM = pl.BlockSpec(memory_space=pltpu.VMEM)
ANY = pl.BlockSpec(memory_space=pltpu.HBM)
f32, bf16 = jnp.float32, jnp.bfloat16


def fit_half_circle():
    nodes = np.cos(np.pi * (np.arange(400) + 0.5) / 800.0) * 0.5
    square = nodes * nodes
    fit = np.polynomial.chebyshev.Chebyshev.fit
    root = np.sqrt(2.0)
    sine = fit(square, root * np.sin(np.pi * nodes) / nodes, 3, domain=[0, 0.25], w=nodes)
    cosine = fit(square, root * np.cos(np.pi * nodes), 4, domain=[0, 0.25])
    kind = np.polynomial.Polynomial
    return [[float(c) for c in p.convert(kind=kind).coef] for p in (sine, cosine)]


SINE, COSINE = fit_half_circle()


def horner(coefs, x):
    total = coefs[-1] * x + coefs[-2]
    for c in coefs[-3::-1]:
        total = total * x + c
    return total


def legendre(x):
    return [
        jnp.ones_like(x),
        x,
        0.5 * (3.0 * x * x - 1.0),
        0.5 * (5.0 * x * x * x - 3.0 * x),
    ]


def split(x):
    high = x.astype(bf16)
    low = (x - high.astype(f32)).astype(bf16)
    return high, low


def dot(a, b):
    return jnp.dot(a, b, preferred_element_type=f32)


def tdot(a, b):
    return lax.dot_general(a, b, (((0,), (0,)), ((), ())), preferred_element_type=f32)


def column(pen):
    count = pen.shape[1]
    row = lax.broadcasted_iota(jnp.int32, (count, count), 0)
    col = lax.broadcasted_iota(jnp.int32, (count, count), 1)
    return jnp.sum(jnp.where(row == col, pen[...], 0.0), axis=1, keepdims=True)


def halves(ref, rows):
    return jnp.concatenate([ref[pl.ds(j, rows, 2), :] for j in range(2)], axis=1)


def fit_taps(values):
    gram = [
        [jnp.sum(values[t] * values[s], axis=0, keepdims=True) for s in range(t + 1)]
        for t in range(NTERM)
    ]
    factor = [[None] * NTERM for _ in range(NTERM)]
    for t in range(NTERM):
        for s in range(t + 1):
            rest = gram[t][s]
            for r in range(s):
                rest = rest - factor[t][r] * factor[s][r]
            factor[t][s] = jnp.sqrt(rest) if s == t else rest / factor[s][s]
    half = []
    for t in range(NTERM):
        rest = values[t]
        for s in range(t):
            rest = rest - factor[t][s] * half[s]
        half.append(rest / factor[t][t])
    taps = [None] * NTERM
    for t in reversed(range(NTERM)):
        rest = half[t]
        for s in range(t + 1, NTERM):
            rest = rest - factor[s][t] * taps[s]
        taps[t] = rest / factor[t][t]
    return taps


def step_kernel(
    n_dir, n_chan, group,
    vis_hbm, uv_hbm, lm_hbm, flux_hbm, band_hbm, g_hbm, dual_hbm, poly_hbm, pen_hbm, harm_hbm,
    cut_hbm,
    gains_out, blocks, band_out,
    vis, uv, lm, flux, band, dual, poly, pen_ref, harm, cut,
    b_ref, b_all, pack, src, g, er, ei,
    erh, erl, eih, eil, nih, nil,
    frh, frl, fih, fil, drh, drl, srh, srl,
    partial, partner,
    rs, power, ones, xs, sums, tcol, goal, offset, hm,
    packed, zin, part, gains,
    ins, gs, gr, ms, mr, bs, br, s1, r1, s3, r3, outs,
):
    rows2, stations = g.shape
    clusters = rows2 // 2
    sources = er.shape[0] // clusters
    flat = clusters * sources
    me_d, me_c = lax.axis_index("dir"), lax.axis_index("chan")
    barrier = pltpu.get_barrier_semaphore()
    members = n_dir * n_chan

    def everyone(body):
        if members <= 64:
            for i in range(1, members):
                body(i // n_chan, i % n_chan)
        else:

            def step(i, carry):
                body(i // n_chan, i % n_chan)
                return carry

            lax.fori_loop(1, members, step, 0)

    for j in range(1, n_dir):
        pl.semaphore_signal(
            barrier, inc=1, device_id={"dir": lax.rem(me_d + j, n_dir)}, device_id_type=MESH
        )
    for j in range(1, n_chan):
        pl.semaphore_signal(
            barrier, inc=1, device_id={"chan": lax.rem(me_c + j, n_chan)}, device_id_type=MESH
        )
    loads = [
        pltpu.make_async_copy(a, b, ins.at[i])
        for i, (a, b) in enumerate(
            [
                (band_hbm, band),
                (lm_hbm, lm),
                (flux_hbm, flux),
                (g_hbm, pack.at[0, : 4 * clusters]),
                (uv_hbm, uv),
                (cut_hbm, cut),
                (dual_hbm, dual),
                (poly_hbm, poly),
                (pen_hbm, pen_ref),
                (harm_hbm, harm),
                (vis_hbm, vis),
            ]
        )
    ]
    for c in loads:
        c.start()

    def send(s, d, a, b, peer):
        return pltpu.make_async_remote_copy(
            src_ref=s, dst_ref=d, send_sem=a, recv_sem=b, device_id=peer, device_id_type=MESH
        )

    row = lax.broadcasted_iota(jnp.int32, ones.shape, 0)
    col = lax.broadcasted_iota(jnp.int32, ones.shape, 1)
    ones[...] = jnp.where(lax.rem(row, clusters) == col // 128, 1.0, 0.0).astype(bf16)
    for c in loads[:5]:
        c.wait()
    table = jnp.concatenate([lm[0], lm[1], jnp.sqrt(flux[...])], axis=0)
    fill = (-3 * clusters) % 128
    table = jnp.concatenate([table, jnp.zeros((fill, sources), f32)], axis=0)
    pack[0, 4 * clusters : 4 * clusters + sources, :] = jnp.transpose(table)
    here = jnp.full((1, 1), band[0], f32)
    b_ref[...] = jnp.full(b_ref.shape, band[0], f32)
    b_all[0] = b_ref[...]
    stretch = 1.0 + 0.25 * here
    u = uv[0:1, :] * stretch
    v = uv[1:2, :] * stretch

    def open_pack(slot):
        g_all = halves(pack.at[slot, : 4 * clusters], rows2)
        g[...] = g_all
        t = pack[slot, 4 * clusters : 4 * clusters + sources, :]
        for k in range(clusters):
            src[k * sources : (k + 1) * sources, :] = pltpu.roll(t, (128 - k) % 128, 1)
        return g_all

    chunk = 4
    span = chunk * sources

    def circle(start):
        cols = src[pl.ds(start, span), :]
        turns = cols[:, 0:1] * u + cols[:, clusters : clusters + 1] * v
        r = turns - jnp.round(turns)
        square = r * r
        s = r * horner(SINE, square)
        c = horner(COSINE, square)
        w = cols[:, 2 * clusters : 2 * clusters + 1]
        ws = w * s
        return w - ws * s, ws * c

    def times(e_r, e_i, c, ref):
        f_r, f_i = [], []
        for i in range(chunk):
            a = ref[pl.ds(c * chunk + i, 1), :]
            b = ref[pl.ds(clusters + c * chunk + i, 1), :]
            p_r = e_r[i * sources : (i + 1) * sources]
            p_i = e_i[i * sources : (i + 1) * sources]
            f_r.append(p_r * a - p_i * b)
            f_i.append(p_r * b + p_i * a)
        return jnp.concatenate(f_r, axis=0), jnp.concatenate(f_i, axis=0)

    def put(h_ref, l_ref, start, x):
        h, l = split(x)
        h_ref[pl.ds(start, span), :] = h
        l_ref[pl.ds(start, span), :] = l
        return h, l

    def field_chunk(c, keep):
        start = c * span if isinstance(c, int) else pl.multiple_of(c * span, span)
        e_r, e_i = circle(start)
        if keep:
            er[pl.ds(start, span), :] = e_r
            ei[pl.ds(start, span), :] = e_i
            put(erh, erl, start, e_r)
            h, l = put(eih, eil, start, e_i)
            nih[pl.ds(start, span), :] = -h
            nil[pl.ds(start, span), :] = -l
        f_r, f_i = times(e_r, e_i, c, g)
        off = 0 if keep else flat
        put(frh, frl, start + off, f_r)
        put(fih, fil, start + off, f_i)
        put(drh, drl, start, f_r - f_i)
        put(srh, srl, start, f_i + f_r)

    lane = lax.broadcasted_iota(jnp.int32, (stations, 128), 1)

    def power_chunk(c):
        acc = tcol[...]
        for i in range(chunk):
            k = c * chunk + i
            at = k * sources
            at = pl.ds(at if isinstance(k, int) else pl.multiple_of(at, sources), sources)
            r_h, r_l, i_h, i_l = erh[at, :], erl[at, :], eih[at, :], eil[at, :]
            n_h, n_l = nih[at, :], nil[at, :]
            left = jnp.concatenate([r_h, i_h, r_h, i_h, r_l, i_l], axis=0)
            real = jnp.concatenate([r_h, i_h, r_l, i_l, r_h, i_h], axis=0)
            imag = jnp.concatenate([n_h, r_h, n_l, r_l, n_h, r_h], axis=0)
            both = tdot(left, jnp.concatenate([real, imag], axis=1))
            c_r, c_i = both[:, :stations], both[:, stations:]
            w = c_r * c_r + c_i * c_i
            power[k] = w
            t = jnp.sum(w * xs[pl.ds(k, 1), :], axis=1, keepdims=True)
            acc = jnp.where(lane == k, t, acc)
        tcol[...] = acc

    def chunks(body, low=0, high=clusters // chunk):
        def step(c, carry):
            body(c)
            return carry

        lax.fori_loop(low, high, step, 0)

    def model(off):
        def rows(a, b):
            return jnp.concatenate([a[off : off + flat, :], b[off : off + flat, :]], axis=0)

        d_h = jnp.concatenate([drh[...], srh[...]], axis=0)
        d_l = jnp.concatenate([drl[...], srl[...]], axis=0)
        first = tdot(rows(frh, fih), jnp.concatenate([d_h, d_l], axis=1))
        second = tdot(rows(frl, fil), d_h)
        return first[:, :stations] + first[:, stations:] + second

    g_own = open_pack(0)
    g_r, g_i = g_own[:clusters], g_own[clusters:]
    xs[:clusters, :] = g_r * g_r + g_i * g_i
    tcol[...] = jnp.zeros((stations, 128), f32)

    pl.semaphore_wait(barrier, n_dir + n_chan - 2)
    per = n_dir // group
    gathers = []
    for j in range(1, per):
        peer = {"dir": lax.rem(me_d + n_dir - group * j, n_dir)}
        gathers.append(send(pack.at[0], pack.at[j], gs.at[j], gr.at[j], peer))
    bands = []
    for j in range(1, n_chan):
        peer = {"chan": lax.rem(me_c + n_chan - j, n_chan)}
        bands.append(send(b_ref, b_all.at[j], bs.at[j], br.at[j], peer))
    for c in gathers + bands:
        c.start()

    count = clusters // chunk
    before = min(3, count - 1)
    for c in range(count):
        field_chunk(c, True)
    partial[...] = model(0)
    for c in range(before):
        power_chunk(c)

    def first_other(c):
        field_chunk(c, False)
        power_chunk(c)

    early = max(before, count - 1)
    if per > 1:
        gathers[0].wait_recv()
        open_pack(1)
        for c in range(count):
            field_chunk(c, False)
            if before <= c < early:
                power_chunk(c)
        partial[...] += model(flat)
    else:
        chunks(power_chunk, before, early)

    def others(j, carry):
        for i in range(2, per):

            @pl.when(j == i)
            def _():
                gathers[i - 1].wait_recv()

        open_pack(j)
        chunks(lambda c: field_chunk(c, False))
        partial[...] += model(flat)
        return carry

    if per > 2:
        lax.fori_loop(2, per, others, 0)
    if group == 2:
        mate = {"dir": me_d + 1 - 2 * lax.rem(me_d, 2)}
        swap = send(partial, partner, ms.at[0], mr.at[0], mate)
        swap.start()
    for c in range(early, count):
        power_chunk(c)

    for c in loads[5:10]:
        c.wait()
    level = legendre(here)
    pen = column(pen_ref)
    pull = jnp.concatenate([pen, pen], axis=0)
    tile = 32 * NTERM
    tiles = stations // 32
    row = lax.broadcasted_iota(jnp.int32, (tile, tile), 0)
    col = lax.broadcasted_iota(jnp.int32, (tile, tile), 1)
    pick = jnp.zeros((tile, tile), f32)
    for t in range(NTERM):
        pick = jnp.where(row - NTERM * col == t, level[t], pick)
    p_h, p_l = split(pick)
    q_h, q_l = split(
        jnp.concatenate([poly[:, j * tile : (j + 1) * tile] for j in range(tiles)], axis=0)
    )
    value = dot(
        jnp.concatenate([q_h, q_l, q_h], axis=1), jnp.concatenate([p_h, p_h, p_l], axis=0)
    )
    value = jnp.concatenate(
        [value[j * rows2 : (j + 1) * rows2, :32] for j in range(tiles)], axis=1
    )
    offset[...] = halves(dual, rows2) / pull
    goal[...] = (value - offset[...]) * pull
    modes = harm.shape[1]

    def mode_block(a):
        start = lax.rem(me_d + a, n_dir) * clusters
        return harm[pl.ds(pl.multiple_of(start, clusters), clusters), :]

    mode_rows = hm.shape[0]
    turned = jnp.concatenate([mode_block(a) for a in range(n_dir)], axis=0)
    turned = jnp.concatenate(
        [turned, jnp.zeros((turned.shape[0], mode_rows - modes), f32)], axis=1
    )
    h_h, h_l = split(jnp.transpose(turned))
    hm[...] = jnp.concatenate([h_h, h_h, h_l], axis=1)
    for c in bands:
        c.wait()
    taps = fit_taps(legendre(b_all[:, 0, :]))

    loads[10].wait()
    if group == 2:
        swap.wait()
        both = partial[...] + partner[...]
    else:
        both = partial[...]
    turned = jnp.transpose(both)

    def seen(i):
        return jnp.concatenate(
            [vis[pl.ds(2 * j + i, stations, 4), :] for j in range(2)], axis=1
        )

    r_h, r_l = split(seen(0) - 0.5 * (both + turned))
    i_h, i_l = split(seen(1) - 0.5 * (both - turned))
    rs[0, :, :stations] = r_h
    rs[0, :, stations:] = -i_h
    rs[1, :, :stations] = i_h
    rs[1, :, stations:] = r_h
    rs[2, :, :stations] = r_l
    rs[2, :, stations:] = -i_l
    rs[3, :, :stations] = i_l
    rs[3, :, stations:] = r_l

    def gather_rows():
        a, b = frh[:flat, :], fih[:flat, :]
        y = dot(
            jnp.concatenate([a, b, a, b, frl[:flat, :], fil[:flat, :]], axis=1),
            jnp.concatenate([rs[0], rs[1], rs[2], rs[3], rs[0], rs[1]], axis=0),
        )
        y_r, y_i = y[:, :stations], y[:, stations:]
        e_r, e_i = er[...], ei[...]

        def over(x):
            return jnp.sum(x.reshape(clusters, sources, stations), axis=1)

        return over(e_r * y_r + e_i * y_i), over(e_r * y_i - e_i * y_r)

    n_r, n_i = gather_rows()
    total = jnp.transpose(tcol[...])[:clusters]
    inverse = 1.0 / (total + pen)
    h_r = (n_r + g_r * total + goal[:clusters, :]) * inverse
    h_i = (n_i + g_i * total + goal[clusters:, :]) * inverse
    xs[:clusters, :] = g_r * h_r + g_i * h_i
    xs[clusters:rows2, :] = g_r * h_i - g_i * h_r
    h_2 = h_r * h_r + h_i * h_i
    high = h_2.astype(bf16).astype(f32)
    two = jnp.concatenate([high, h_2 - high], axis=0)
    two = jnp.concatenate([two, jnp.zeros((128 - rows2, stations), f32)], axis=0)
    two = jnp.transpose(two)[:, :rows2].astype(bf16)
    g[:clusters, :] = h_r
    g[clusters:, :] = h_i

    def again(c):
        start = c * span
        at = pl.ds(start, span)
        f_r, f_i = times(er[at, :], ei[at, :], c, g)
        put(frh, frl, start, f_r)
        put(fih, fil, start, f_i)

    for c in range(clusters // chunk):
        again(c)
    spread_2 = dot(two, ones[...])
    m_r, m_i = gather_rows()
    for k in range(clusters):
        w = power[k]
        c = spread_2[:, 128 * k : 128 * k + 128]
        sums[2 * clusters + k : 2 * clusters + k + 1, :] = jnp.concatenate(
            [
                jnp.sum(w[:, 128 * h : 128 * h + 128] * c, axis=0, keepdims=True)
                for h in range(stations // 128)
            ],
            axis=1,
        )
        for i in range(2):
            j = i * clusters + k
            t = w * xs[j : j + 1, :]
            t = sum(t[:, 128 * h : 128 * h + 128] for h in range(1, stations // 128)) + t[:, :128]
            sums[j : j + 1, :] = jnp.sum(jnp.transpose(t), axis=0, keepdims=True)
    t_0, t_1, t_2 = (sums[i * clusters : (i + 1) * clusters, :] for i in range(3))
    inverse = 1.0 / (t_2 + pen)
    new_r = (m_r + g_r * t_0 - g_i * t_1 + goal[:clusters, :]) * inverse
    new_i = (m_i + g_r * t_1 + g_i * t_0 + goal[clusters:, :]) * inverse
    new = jnp.concatenate([new_r, new_i], axis=0)
    gains[...] = new
    emit = pltpu.make_async_copy(gains, gains_out, outs.at[0])
    emit.start()

    spread = new + offset[...]
    each = stations // n_chan
    groups = rows2 // 8
    used = groups * each
    lanes = packed.shape[2]
    for j in range(n_chan):
        if used < lanes:
            packed[j] = jnp.zeros((8, lanes), f32)
        packed[j, :, :used] = jnp.concatenate(
            [spread[8 * i : 8 * i + 8, j * each : (j + 1) * each] for i in range(groups)], axis=1
        )
    def moment(a, j):
        to_d, to_c = lax.rem(me_d + n_dir - a, n_dir), lax.rem(me_c + n_chan - j, n_chan)
        return send(
            packed.at[to_c], zin.at[a, j], s1.at[a, j], r1.at[a, j], {"dir": to_d, "chan": to_c}
        )

    everyone(lambda a, j: moment(a, j).start())
    wide = NTERM * each
    width = part.shape[1]
    rows = []
    for a in range(n_dir):
        mixed = [None] * NTERM
        for j in range(n_chan):
            if a == j == 0:
                got = packed[me_c]
            else:
                moment(a, j).wait_recv()
                got = zin[a, j]
            for t in range(NTERM):
                term = got * taps[t][j : j + 1, 0:1]
                mixed[t] = term if j == 0 else mixed[t] + term

        def terms(i):
            row = [mixed[t][:, i * each : (i + 1) * each] for t in range(NTERM)]
            if wide < width:
                row.append(jnp.zeros((8, width - wide), f32))
            return jnp.concatenate(row, axis=1)

        tall = groups // 2
        rows.append(
            jnp.concatenate(
                [
                    jnp.concatenate([terms(r * tall + i) for i in range(tall)], axis=0)
                    for r in range(2)
                ],
                axis=1,
            )
        )
    z_h, z_l = split(jnp.concatenate(rows, axis=0))
    a = dot(hm[...], jnp.concatenate([z_h, z_l, z_h], axis=0))
    a_r, a_i = a[:, :width], a[:, width:]
    size = jnp.sqrt(a_r * a_r + a_i * a_i)
    limit = cut[0]
    scale = jnp.maximum(size - limit, 0.0) / jnp.maximum(size, limit)
    a_h, a_l = split(jnp.concatenate([a_r * scale, a_i * scale], axis=1)[:modes])
    m_h, m_l = split(mode_block(0))
    twice = dot(jnp.concatenate([m_h, m_l], axis=0), a_h)
    done = twice[:clusters] + twice[clusters:] + dot(m_h, a_l)
    part[:clusters] = done[:, :width]
    part[clusters:] = done[:, width:]
    third = []
    for j in range(1, n_chan):
        peer = lax.rem(me_c + j, n_chan)
        third.append(send(part, blocks.at[me_c], s3.at[j], r3.at[j], {"chan": peer}))
    for c in third:
        c.start()
    keep = pltpu.make_async_copy(part, blocks.at[me_c], outs.at[1])
    keep.start()
    show = pltpu.make_async_copy(b_ref, band_out, outs.at[2])
    show.start()
    for c in gathers:
        c.wait_send()
    everyone(lambda a, j: moment(a, j).wait_send())
    emit.wait()
    keep.wait()
    show.wait()
    for c in third:
        c.wait()


def emit_kernel(
    blocks_hbm, gains_hbm, dual_hbm, pen_hbm, band_hbm, gains_hbm_out, dual_hbm_out, cons_hbm_out,
    blocks, gains, dual, pen_ref, band, gains_out, dual_out, cons_out, ins, outs,
):
    pairs = [
        (blocks_hbm, blocks), (band_hbm, band), (gains_hbm, gains), (dual_hbm, dual),
        (pen_hbm, pen_ref),
    ]
    loads = [pltpu.make_async_copy(x, y, ins.at[i]) for i, (x, y) in enumerate(pairs)]
    for c in loads:
        c.start()
    pairs = [(gains_out, gains_hbm_out), (cons_out, cons_hbm_out), (dual_out, dual_hbm_out)]
    stores = [pltpu.make_async_copy(x, y, outs.at[i]) for i, (x, y) in enumerate(pairs)]
    n_chan, rows2, width = blocks.shape
    stations = gains.shape[1]
    each = stations // n_chan
    wide = NTERM * each
    loads[1].wait()
    level = legendre(band[0:1, 0:1])
    row = lax.broadcasted_iota(jnp.int32, (width, width), 0)
    col = lax.broadcasted_iota(jnp.int32, (width, width), 1)
    weave = jnp.zeros((width, width), f32)
    sample = jnp.zeros((width, width), f32)
    for t in range(NTERM):
        place = row - t * each
        inside = (place >= 0) & (place < each)
        weave = jnp.where(inside & (col == NTERM * place + t), 1.0, weave)
        sample = jnp.where(inside & (col == place), level[t], sample)
    s_h, s_l = split(sample)
    both = jnp.concatenate([weave.astype(bf16), s_h], axis=1)
    rest = jnp.concatenate([jnp.zeros((width, width), bf16), s_l], axis=1)
    for c in loads[2:] + loads[:1]:
        c.wait()
    pen = column(pen_ref)
    pull = jnp.concatenate([pen, pen], axis=0)
    new = gains[...]
    for j in range(2):
        gains_out[pl.ds(j, rows2, 2), :] = new[:, j * 128 : (j + 1) * 128]
    stores[0].start()
    b_h, b_l = split(jnp.concatenate([blocks[j] for j in range(n_chan)], axis=0))
    result = dot(
        jnp.concatenate([b_h, b_l, b_h], axis=1), jnp.concatenate([both, both, rest], axis=0)
    )
    fitted = []
    for j in range(n_chan):
        piece = result[j * rows2 : (j + 1) * rows2]
        cons_out[:, j * wide : (j + 1) * wide] = piece[:, :wide]
        fitted.append(piece[:, width : width + each])
    stores[1].start()
    fitted = jnp.concatenate(fitted, axis=1)
    fresh = halves(dual, rows2) + pull * (new - fitted)
    for j in range(2):
        dual_out[pl.ds(j, rows2, 2), :] = fresh[:, j * 128 : (j + 1) * 128]
    stores[2].start()
    for c in stores:
        c.wait()


def solution(mesh):
    n_dir, n_chan = mesh.shape["dir"], mesh.shape["chan"]
    group = 2 if n_dir % 2 == 0 else 1

    def shards(
        visibilities, station_uv, source_lm, source_flux, band_offset, gains_init, duals_init,
        poly_init, penalty, harmonics, threshold,
    ):
        _, clusters, sources = source_lm.shape
        stations = station_uv.shape[1]
        modes = harmonics.shape[1]
        mode_rows = -(-modes // 128) * 128
        rows2 = 2 * clusters
        lanes = max(128, stations * NTERM // n_chan)
        flat = clusters * sources
        small = max(128, stations // n_chan * (rows2 // 8))
        vis = visibilities.reshape(stations, 2, stations // 128, 128)
        vis = vis.transpose(0, 2, 1, 3).reshape(stations * 4, 128)
        lines = rows2 * stations // 128
        dual = duals_init.reshape(lines, 128)
        pen = penalty.reshape(1, clusters)
        dma = pltpu.SemaphoreType.DMA
        vm = pltpu.VMEM
        wide16 = vm((flat, stations), bf16)
        long16 = vm((2 * flat, stations), bf16)
        per = n_dir // group
        gains, blocks, band = pl.pallas_call(
            functools.partial(step_kernel, n_dir, n_chan, group),
            out_shape=(
                jax.ShapeDtypeStruct((rows2, stations), f32),
                jax.ShapeDtypeStruct((n_chan, rows2, lanes), f32),
                jax.ShapeDtypeStruct((8, 128), f32),
            ),
            in_specs=[ANY] * 11,
            out_specs=(ANY,) * 3,
            scratch_shapes=[
                vm((stations * 4, 128), f32),
                vm(station_uv.shape, f32),
                vm(source_lm.shape, f32),
                vm(source_flux.shape, f32),
                pltpu.SMEM((1,), f32),
                vm((lines, 128), f32),
                vm((rows2, stations * NTERM), f32),
                vm(pen.shape, f32),
                vm(harmonics.shape, f32),
                pltpu.SMEM((1,), f32),
                vm((8, 128), f32),
                vm((n_chan, 8, 128), f32),
                vm((per, lines + sources, 128), f32),
                vm((flat, 128), f32),
                vm((rows2, stations), f32),
                vm((flat, stations), f32),
                vm((flat, stations), f32),
                wide16, wide16, wide16, wide16, wide16, wide16,
                long16, long16, long16, long16,
                wide16, wide16, wide16, wide16,
                vm((stations, stations), f32),
                vm((stations, stations), f32),
                vm((4, stations, 2 * stations), bf16),
                vm((clusters, stations, stations), f32),
                vm((rows2, clusters * 128), bf16),
                vm((rows2, stations), f32),
                vm((3 * clusters, stations), f32),
                vm((stations, 128), f32),
                vm((rows2, stations), f32),
                vm((rows2, stations), f32),
                vm((mode_rows, 3 * harmonics.shape[0]), bf16),
                vm((n_chan, 8, small), f32),
                vm((n_dir, n_chan, 8, small), f32),
                vm((rows2, lanes), f32),
                vm((rows2, stations), f32),
                dma((11,)),
                dma((per,)), dma((per,)),
                dma((1,)), dma((1,)),
                dma((n_chan,)), dma((n_chan,)),
                dma((n_dir, n_chan)), dma((n_dir, n_chan)),
                dma((n_chan,)), dma((n_chan,)),
                dma((3,)),
            ],
            compiler_params=pltpu.CompilerParams(
                collective_id=0, has_side_effects=True, vmem_limit_bytes=62 * 2**20
            ),
            name="calibrate",
        )(
            vis, station_uv, source_lm, source_flux, band_offset, gains_init.reshape(lines, 128), dual,
            poly_init.reshape(rows2, stations * NTERM), pen, harmonics, threshold,
        )
        gains, duals, consensus = pl.pallas_call(
            emit_kernel,
            out_shape=(
                jax.ShapeDtypeStruct((lines, 128), f32),
                jax.ShapeDtypeStruct((lines, 128), f32),
                jax.ShapeDtypeStruct((rows2, stations * NTERM), f32),
            ),
            in_specs=[ANY] * 5,
            out_specs=(ANY,) * 3,
            scratch_shapes=[
                vm((n_chan, rows2, lanes), f32),
                vm((rows2, stations), f32),
                vm((lines, 128), f32),
                vm(pen.shape, f32),
                vm((8, 128), f32),
                vm((lines, 128), f32),
                vm((lines, 128), f32),
                vm((rows2, stations * NTERM), f32),
                dma((5,)),
                dma((3,)),
            ],
            compiler_params=pltpu.CompilerParams(vmem_limit_bytes=62 * 2**20),
            name="emit",
        )(blocks, gains, dual, pen, band)
        shape = (2, clusters, 1, stations)
        return (
            gains.reshape(shape),
            duals.reshape(shape),
            consensus.reshape(2, clusters, stations * NTERM),
        )

    return jax.shard_map(
        shards,
        mesh=mesh,
        in_specs=(
            P("chan", None, None, None),
            P(),
            P(None, "dir", None),
            P("dir", None),
            P("chan"),
            P(None, "dir", "chan", None),
            P(None, "dir", "chan", None),
            P(None, "dir", None),
            P("dir"),
            P(),
            P(),
        ),
        out_specs=(
            P(None, "dir", "chan", None),
            P(None, "dir", "chan", None),
            P(None, "dir", None),
        ),
        check_vma=False,
    )
```
